256 devices in a mesh: grp: 4 (over y), dev: 64 (over z, x, core).
Axes of the slice: x: 4, y: 4, z: 8, core: 2. Of those that a mesh axis runs over, the one named last changes fastest.
Arguments:
- leaf_inverse: float32 [196608, 768], P(('grp', 'dev')), as said below
- leaf_basis: float32 [196608, 256], P(('grp', 'dev')), may hold values from -0.3125 to 0.3125
- node_block: float32 [524288, 256], P(('grp', 'dev')), as said below
- node_link: float32 [524288, 256], P(('grp', 'dev')), as said below
- loads: float32 [196608, 128], P(('grp', 'dev')), may hold values from -6 to 6
- order: int32 [256, 768], P(('grp', 'dev')), may hold values from 0 to 767, each once within a row
Outputs:
- solution: float32 [196608, 128], P(('grp', 'dev'))
The draws below stay inside these ranges and needn't reach their ends.
Inputs may be any that keep to these rules, and one draw needn't show every extreme that they name: `leaf_inverse`: each leaf's block is symmetric with a positive diagonal plus a positive semidefinite part. `node_block`: each block is symmetric with a positive diagonal plus a positive semidefinite part; leaves below the same node of level k hold equal blocks for level k. `node_link`: leaves below the same node of level k hold equal blocks for level k. `order`: each row is a permutation of 0 to 767.
All inputs are finite; a program needn't handle non-finite values.
Results may differ from the reference program's by a relative error of at most 0.0001.
Values sent between devices are 32-bit elements; how exact they have to be, the bound alone decides.
A program may use at most 128 MiB of HBM per device.

```python
import math
import jax
import jax.numpy as jnp
import numpy as np
from jax import lax

LEAF = 768
SKELETON_RANK = 256
NRHS = 128
LEAVES = 256
LEVELS = 8
SYSTEM = 196608


def spd_blocks(key, number, order_size, lo_value, hi_value, coupling):
    first, second = jax.random.split(key)
    diag_part = jax.random.uniform(first, (number, order_size), minval=lo_value, maxval=hi_value)
    rough = jax.random.normal(second, (number, order_size, order_size), dtype=jnp.float32)
    product = jnp.einsum('nab,ncb->nac', rough, rough, precision=lax.Precision.HIGHEST) * (coupling / order_size)
    product = 0.5 * (product + jnp.swapaxes(product, 1, 2))
    eye_mat = jnp.eye(order_size, dtype=jnp.float32)
    return product + diag_part[:, :, None] * eye_mat[None, :, :]


def ancestor_table():
    leaf_ids = np.arange(LEAVES)
    columns = []
    for level in range(1, LEVELS + 1):
        columns.append((leaf_ids >> level) * 2 ** level + 2 ** (level - 1))
    return np.stack(columns, axis=1)


def draw_leaf_inverse(key, part):
    blocks = spd_blocks(jax.random.fold_in(key, 11), LEAVES, LEAF, 0.5, 1.0, 0.25)
    return blocks.reshape(LEAVES * LEAF, LEAF).astype(jnp.float32)


def draw_node_block(key, part):
    blocks = spd_blocks(jax.random.fold_in(key, 23), LEAVES, SKELETON_RANK, 0.2, 0.6, 0.1)
    placed = blocks[ancestor_table()]
    return placed.reshape(LEAVES * LEVELS * SKELETON_RANK, SKELETON_RANK).astype(jnp.float32)


def draw_node_link(key, part):
    raw = jax.random.normal(jax.random.fold_in(key, 37), (LEAVES, SKELETON_RANK, SKELETON_RANK), dtype=jnp.float32)
    raw = raw * (1.0 / math.sqrt(SKELETON_RANK))
    placed = raw[ancestor_table()]
    return placed.reshape(LEAVES * LEVELS * SKELETON_RANK, SKELETON_RANK).astype(jnp.float32)


def steps_of(key, dims, cuts, least, high):
    level, own = 1.0, jax.random.fold_in(key, 6)
    for position, parts in cuts:
        heights = jnp.exp(jax.random.uniform(jax.random.fold_in(own, position), (parts,), jnp.float32, least / len(cuts), high / len(cuts)))
        level = level * jnp.repeat(heights, dims[position] // parts).reshape([-1 if axis == position else 1 for axis in range(len(dims))])
    return level


def normal_values(key, extent, spread, bound, pieces=(), held_as=jnp.bfloat16):
    array = jax.random.normal(key, extent, jnp.float32) * spread
    if len(pieces) > 0:
        array = steps_of(key, extent, pieces, -0.22, 0.18) * array
    return jnp.clip(array, min=-bound, max=bound).astype(held_as)


def setup_inputs(seed: int = 0) -> dict:
    splits = jax.random.split(jax.random.key(seed), 7)
    leaf_inverse = draw_leaf_inverse(jax.random.fold_in(splits[6], 71), 0)
    leaf_basis = normal_values(splits[1], (SYSTEM, SKELETON_RANK), (LEAF // 2) ** -0.5, 0.3125, ((0, 256),), jnp.float32)
    node_block = draw_node_block(jax.random.fold_in(splits[6], 71), 0)
    node_link = draw_node_link(jax.random.fold_in(splits[6], 71), 0)
    loads = normal_values(splits[4], (SYSTEM, NRHS), 1.0, 6.0, ((0, 256),), jnp.float32)
    order = jax.vmap(lambda own: jax.random.permutation(own, LEAF))(jax.random.split(splits[5], LEAVES)).reshape((LEAVES, LEAF)).astype(jnp.int32)
    return dict(leaf_inverse=leaf_inverse, leaf_basis=leaf_basis, node_block=node_block, node_link=node_link, loads=loads, order=order)


def reference(leaf_inverse, leaf_basis, node_block, node_link, loads, order):
    topmost_level = lax.Precision.HIGHEST
    count = LEAVES
    levels = LEVELS
    inverses = leaf_inverse.reshape(count, LEAF, LEAF)
    skeleton_basis = leaf_basis.reshape(count, LEAF, SKELETON_RANK)
    nodes = node_block.reshape(count, levels, SKELETON_RANK, SKELETON_RANK)
    links = node_link.reshape(count, levels, SKELETON_RANK, SKELETON_RANK)
    index_full = jnp.broadcast_to(order[:, :, None], (count, LEAF, NRHS))
    rows = jnp.take_along_axis(loads.reshape(count, LEAF, NRHS), index_full, axis=1)
    leaf_solution = jnp.einsum('eab,ebc->eac', inverses, jnp.concatenate([skeleton_basis, rows], axis=2), precision=topmost_level)
    lifted_rows = jnp.einsum('eqd,eqc->edc', skeleton_basis, leaf_solution, precision=topmost_level)
    stored = []
    for level in range(1, levels + 1):
        heads = np.arange(count >> level) * 2 ** level
        sign = -1.0 if level % 2 else 1.0
        factor = nodes[heads, level - 1] + lifted_rows[0::2, :, :SKELETON_RANK] + lifted_rows[1::2, :, :SKELETON_RANK]
        target = -sign * (lifted_rows[0::2, :, SKELETON_RANK:] + lifted_rows[1::2, :, SKELETON_RANK:])
        chol_node = jnp.linalg.cholesky(factor)
        link_now = links[heads, level - 1]
        solved = jax.scipy.linalg.cho_solve((chol_node, True), jnp.concatenate([link_now, target], axis=2))
        lifted_rows = jnp.einsum('nrs,nrt->nst', link_now, solved, precision=topmost_level)
        stored.append(solved)
    value = stored[-1][:, :, SKELETON_RANK:]
    for level in range(levels, 1, -1):
        solved = stored[level - 2]
        sign = -1.0 if (level - 1) % 2 else 1.0
        ancestor_part = jnp.repeat(value, 2, axis=0)
        value = solved[:, :, SKELETON_RANK:] - sign * jnp.einsum('nrs,nst->nrt', solved[:, :, :SKELETON_RANK], ancestor_part, precision=topmost_level)
    ancestor_part = jnp.repeat(value, 2, axis=0)
    local_part = leaf_solution[:, :, SKELETON_RANK:] - jnp.einsum('oha,oan->ohn', leaf_solution[:, :, :SKELETON_RANK], ancestor_part, precision=topmost_level)
    leaf_ids = jnp.arange(count, dtype=jnp.int32)[:, None]
    solution = jnp.zeros_like(local_part).at[leaf_ids, order.astype(jnp.int32)].set(local_part)
    return solution.reshape(count * LEAF, NRHS)
```

```python
import functools
import jax
import jax.numpy as jnp
from jax import lax
from jax.experimental import pallas as pl
from jax.experimental.pallas import tpu as pltpu
from jax.sharding import PartitionSpec as P

BF = jnp.bfloat16
F32 = jnp.float32
MESH = pl.DeviceIdType.MESH
HALF = 128
RANK = 256
NRHS = 128
LEAF = 768
LEVELS = 8
WIDE = RANK + NRHS
TERMS = ((0, 0), (0, 1), (1, 0), (0, 2), (2, 0), (1, 1))


def dot(a, b):
    return jnp.dot(a, b, precision=lax.Precision.HIGHEST, preferred_element_type=F32)


def dot_tn(a, b):
    return lax.dot_general(
        a, b, (((0,), (0,)), ((), ())), precision=lax.Precision.HIGHEST, preferred_element_type=F32
    )


def parts_of(x):
    high = x.astype(BF).astype(F32)
    rest = x - high
    mid = rest.astype(BF).astype(F32)
    return (high, mid, rest - mid)


def rank8_product(rows, solved):
    a, b = parts_of(rows), parts_of(solved)
    left = jnp.concatenate([a[i] for i, _ in TERMS], axis=0).astype(BF)
    right = jnp.concatenate([b[j] for _, j in TERMS], axis=0).astype(BF)
    return lax.dot_general(left, right, (((0,), (0,)), ((), ())), preferred_element_type=F32)


def sweep(a_ref):
    size = a_ref.shape[0]
    tile = (8, size)
    lane = lax.broadcasted_iota(jnp.int32, tile, 1)
    sub = lax.broadcasted_iota(jnp.int32, tile, 0)

    def spread(v):
        return jnp.broadcast_to(v, tile)

    now = a_ref[0:8, :]
    for first in range(0, size, 8):
        here = (lane >= first) & (lane < first + 8)
        columns = [spread(now[:, first + j : first + j + 1]) for j in range(8)]
        entry = {(i, j): spread(columns[j][i : i + 1, :]) for j in range(8) for i in range(j, 8)}
        row = [
            jnp.where(here, jnp.where(lane == first + i, -1.0, 0.0), spread(now[i : i + 1, :]))
            for i in range(8)
        ]
        lower, pivot = {}, []
        for k in range(8):
            pivot.append(1.0 / entry[k, k])
            for i in range(k + 1, 8):
                lower[i, k] = entry[i, k] * pivot[k]
            for i in range(k + 1, 8):
                for j in range(k + 1, i + 1):
                    entry[i, j] = entry[i, j] - lower[i, k] * entry[j, k]
                row[i] = row[i] - lower[i, k] * row[k]
        row = [r * p for r, p in zip(row, pivot)]
        for k in range(7, -1, -1):
            for i in range(k):
                row[i] = row[i] - lower[k, i] * row[k]
        solved = row[7]
        for i in range(7):
            solved = jnp.where(sub == i, row[i], solved)
        change = rank8_product(now, solved)
        after = None
        if first + 8 < size:
            after = a_ref[first + 8 : first + 16, :]
            terms = [spread(after[:, first + i : first + i + 1]) * row[i] for i in range(8)]
            while len(terms) > 1:
                terms = [terms[q] + terms[q + 1] for q in range(0, len(terms), 2)]
            after = jnp.where(here, 0.0, after) - terms[0]
        for q in range(0, size, 8):
            if q == first:
                a_ref[q : q + 8, :] = solved
            elif q == first + 8:
                a_ref[q : q + 8, :] = after
            else:
                old = jnp.where(here, 0.0, a_ref[q : q + 8, :])
                a_ref[q : q + 8, :] = old - change[q : q + 8, :]
        now = after


PIECES = (
    (slice(0, 128), slice(0, 128)),
    (slice(0, 128), slice(128, 256)),
    (slice(128, 256), slice(128, 256)),
    (slice(0, 256), slice(256, 384)),
)


def partner_of(level):
    dev, grp = lax.axis_index("dev"), lax.axis_index("grp")
    core, x, z = dev % 2, (dev // 2) % 4, dev // 8
    one = lambda flag, yes, no: jnp.where(flag, yes, no)
    new_core = one(level == 1, 1 - core, core)
    flip_x = x + 1 - 2 * (x % 2)
    new_x = one(level == 2, flip_x, one(level == 3, 3 - x, x))
    flip_z0 = z + 1 - 2 * (z % 2)
    flip_z1 = z + 2 - 4 * ((z // 2) % 2)
    new_z = one(level == 4, flip_z0, one(level == 5, flip_z1, one(level == 6, 7 - z, z)))
    flip_y = grp + 1 - 2 * (grp % 2)
    new_y = one(level == 7, flip_y, one(level == 8, 3 - grp, grp))
    return (new_y, (new_z * 4 + new_x) * 2 + new_core)


def kernel(
    inverse_hbm, basis_hbm, block_hbm, link_hbm, loads_hbm, order_ref, out_hbm,
    inverse, basis, block, link, loads, hot, leaf_w, leaf_y, lift, received, gain, part, value, low, high, result,
    in_sem, send_sem, recv_sem, out_sem,
):
    loaded = []
    for i, (src, dst) in enumerate(
        [(basis_hbm, basis), (inverse_hbm, inverse), (loads_hbm, loads), (block_hbm, block), (link_hbm, link)]
    ):
        loaded.append(pltpu.make_async_copy(src, dst, in_sem.at[i]))
        loaded[-1].start()
    barrier = pltpu.get_barrier_semaphore()
    for level in range(1, LEVELS + 1):
        pl.semaphore_signal(barrier, inc=1, device_id=partner_of(level), device_id_type=MESH)

    def exchange(level, piece):
        rows, columns = PIECES[piece]
        return pltpu.make_async_remote_copy(
            src_ref=lift.at[rows, columns],
            dst_ref=received.at[level - 1, rows, columns],
            send_sem=send_sem.at[level - 1, piece],
            recv_sem=recv_sem.at[level - 1, piece],
            device_id=partner_of(level),
            device_id_type=MESH,
        )

    loaded[0].wait()
    loaded[1].wait()
    leaf_w[...] = dot(inverse[...], basis[...])
    upper = dot_tn(basis[...], leaf_w[...])
    lift[:, :RANK] = upper
    pl.semaphore_wait(barrier, LEVELS)
    for piece in range(3):
        exchange(1, piece).start()
    loaded[2].wait()
    rows = lax.broadcasted_iota(jnp.int32, (LEAF, LEAF), 0)
    hot[...] = jnp.where(rows == order_ref[...], 1.0, 0.0).astype(BF)
    pieces = parts_of(loads[...])
    stacked = jnp.concatenate([p.astype(BF) for p in pieces], axis=1)
    picked = lax.dot_general(hot[...], stacked, (((0,), (0,)), ((), ())), preferred_element_type=F32)
    reordered = (picked[:, :NRHS] + picked[:, NRHS : 2 * NRHS]) + picked[:, 2 * NRHS :]
    leaf_y[...] = dot(inverse[...], reordered)
    lift[:, RANK:] = dot_tn(basis[...], leaf_y[...])
    exchange(1, 3).start()
    loaded[3].wait()
    loaded[4].wait()

    def node(level, carry):
        slot = level - 1
        base = slot * RANK
        top = pl.ds(pl.multiple_of(base, RANK), HALF)
        bottom = pl.ds(pl.multiple_of(base + HALF, HALF), HALF)

        def joined(rows, columns):
            return lift[rows, columns] + received[slot, rows, columns]

        exchange(level, 0).wait_recv()
        low[...] = block[top, 0:HALF] + joined(*PIECES[0])
        sweep(low)
        for piece in range(1, 4):
            exchange(level, piece).wait_recv()
        sign = 2.0 * (level % 2).astype(F32) - 1.0
        target = sign * joined(*PIECES[3])
        cross = block[top, HALF:RANK] + joined(*PIECES[1])
        first = -low[...]
        through = dot(first, cross)
        high[...] = block[bottom, HALF:RANK] + joined(*PIECES[2]) - dot_tn(cross, through)
        link_low, link_high = link[top, :], link[bottom, :]
        given_low = jnp.concatenate([link_low, target[:HALF]], axis=1)
        given_high = jnp.concatenate([link_high, target[HALF:]], axis=1)
        solved_low = dot(first, given_low)
        rest = given_high - dot_tn(cross, solved_low)
        lifted = dot_tn(link_low, solved_low)
        sweep(high)
        solved_high = dot(-high[...], rest)
        lifted = lifted + dot_tn(rest[:, :RANK], solved_high)
        for piece in range(4):
            exchange(level, piece).wait_send()
        lift[...] = lifted

        @pl.when(level < LEVELS)
        def _():
            for piece in range(4):
                exchange(level + 1, piece).start()

        solved_low = solved_low - dot(through, solved_high)
        gain[slot, 0:HALF, :] = solved_low[:, :RANK]
        gain[slot, HALF:RANK, :] = solved_high[:, :RANK]
        part[slot, 0:HALF, :] = solved_low[:, RANK:]
        part[slot, HALF:RANK, :] = solved_high[:, RANK:]
        return carry

    lax.fori_loop(1, LEVELS + 1, node, 0)

    value[...] = part[LEVELS - 1]

    def down(step, carry):
        level = LEVELS - 1 - step
        sign = 1.0 - 2.0 * (level % 2).astype(F32)
        value[...] = part[level - 1] - sign * dot(gain[level - 1], value[...])
        return carry

    lax.fori_loop(0, LEVELS - 1, down, 0)
    local = leaf_y[...] - dot(leaf_w[...], value[...])
    stacked = jnp.concatenate([p.astype(BF) for p in parts_of(local)], axis=1)
    placed = jnp.dot(hot[...], stacked, preferred_element_type=F32)
    result[...] = (placed[:, :NRHS] + placed[:, NRHS : 2 * NRHS]) + placed[:, 2 * NRHS :]
    done = pltpu.make_async_copy(result, out_hbm, out_sem)
    done.start()
    done.wait()


def shards(leaf_inverse, leaf_basis, node_block, node_link, loads, order):
    hbm = pl.BlockSpec(memory_space=pl.ANY)
    return pl.pallas_call(
        kernel,
        out_shape=jax.ShapeDtypeStruct(loads.shape, F32),
        in_specs=[hbm] * 5 + [pl.BlockSpec(memory_space=pltpu.VMEM)],
        out_specs=hbm,
        scratch_shapes=[
            pltpu.VMEM((LEAF, LEAF), F32),
            pltpu.VMEM((LEAF, RANK), F32),
            pltpu.VMEM((LEVELS * RANK, RANK), F32),
            pltpu.VMEM((LEVELS * RANK, RANK), F32),
            pltpu.VMEM((LEAF, NRHS), F32),
            pltpu.VMEM((LEAF, LEAF), BF),
            pltpu.VMEM((LEAF, RANK), F32),
            pltpu.VMEM((LEAF, NRHS), F32),
            pltpu.VMEM((RANK, WIDE), F32),
            pltpu.VMEM((LEVELS, RANK, WIDE), F32),
            pltpu.VMEM((LEVELS, RANK, RANK), F32),
            pltpu.VMEM((LEVELS, RANK, NRHS), F32),
            pltpu.VMEM((RANK, NRHS), F32),
            pltpu.VMEM((HALF, HALF), F32),
            pltpu.VMEM((HALF, HALF), F32),
            pltpu.VMEM((LEAF, NRHS), F32),
            pltpu.SemaphoreType.DMA((5,)),
            pltpu.SemaphoreType.DMA((LEVELS, 4)),
            pltpu.SemaphoreType.DMA((LEVELS, 4)),
            pltpu.SemaphoreType.DMA,
        ],
        compiler_params=pltpu.CompilerParams(
            collective_id=0, has_side_effects=True, vmem_limit_bytes=48 * 1024 * 1024
        ),
        cost_estimate=pl.CostEstimate(flops=4_000_000_000, bytes_accessed=8_000_000, transcendentals=0),
    )(leaf_inverse, leaf_basis, node_block, node_link, loads, order)


def solution(mesh):
    spec = P(("grp", "dev"), None)
    return jax.shard_map(shards, mesh=mesh, in_specs=(spec,) * 6, out_specs=spec, check_vma=False)
```

```python
import functools
import jax
import jax.numpy as jnp
from jax import lax
from jax.experimental import pallas as pl
from jax.experimental.pallas import tpu as pltpu
from jax.sharding import PartitionSpec as P

BF = jnp.bfloat16
F32 = jnp.float32
MESH = pl.DeviceIdType.MESH
HALF = 128
RANK = 256
NRHS = 128
LEAF = 768
LEVELS = 8
WIDE = RANK + NRHS
TERMS = ((0, 0), (0, 1), (1, 0), (0, 2), (2, 0), (1, 1))


def halves(x):
    high = x.astype(BF)
    return high, (x - high.astype(F32)).astype(BF)


def dot(a, b):
    ah, al = halves(a)
    bh, bl = halves(b)
    one = lambda p, q: jnp.dot(p, q, preferred_element_type=F32)
    return one(ah, bh) + (one(ah, bl) + one(al, bh))


def dot_tn(a, b):
    ah, al = halves(a)
    bh, bl = halves(b)
    one = lambda p, q: lax.dot_general(p, q, (((0,), (0,)), ((), ())), preferred_element_type=F32)
    return one(ah, bh) + (one(ah, bl) + one(al, bh))


def dot_tn_exact(a, b):
    return lax.dot_general(a, b, (((0,), (0,)), ((), ())), preferred_element_type=F32)


def whole(x):
    size = x.shape[1] // 3
    return (x[:, :size] + x[:, size : 2 * size]) + x[:, 2 * size :]


def parts_of(x):
    high = x.astype(BF).astype(F32)
    rest = x - high
    mid = rest.astype(BF).astype(F32)
    return (high, mid, rest - mid)


def rank8_product(rows, solved):
    a, b = parts_of(rows), parts_of(solved)
    left = jnp.concatenate([a[i] for i, _ in TERMS], axis=0).astype(BF)
    right = jnp.concatenate([b[j] for _, j in TERMS], axis=0).astype(BF)
    return lax.dot_general(left, right, (((0,), (0,)), ((), ())), preferred_element_type=F32)


def sweep(a_ref):
    size = a_ref.shape[0]
    tile = (8, size)
    lane = lax.broadcasted_iota(jnp.int32, tile, 1)
    sub = lax.broadcasted_iota(jnp.int32, tile, 0)

    def spread(v):
        return jnp.broadcast_to(v, tile)

    def column(v, j):
        return jnp.take_along_axis(v, jnp.full(tile, j, jnp.int32), axis=1)

    now = a_ref[0:8, :]
    for first in range(0, size, 8):
        here = (lane >= first) & (lane < first + 8)
        columns = [column(now, first + j) for j in range(8)]
        entry = {(i, j): spread(columns[j][i : i + 1, :]) for j in range(8) for i in range(j, 8)}
        row = [
            jnp.where(here, jnp.where(lane == first + i, -1.0, 0.0), spread(now[i : i + 1, :]))
            for i in range(8)
        ]
        lower, pivot = {}, []
        for k in range(8):
            pivot.append(1.0 / entry[k, k])
            for i in range(k + 1, 8):
                lower[i, k] = entry[i, k] * pivot[k]
            for i in range(k + 1, 8):
                for j in range(k + 1, i + 1):
                    entry[i, j] = entry[i, j] - lower[i, k] * entry[j, k]
                row[i] = row[i] - lower[i, k] * row[k]
        row = [r * p for r, p in zip(row, pivot)]
        for k in range(7, -1, -1):
            for i in range(k):
                row[i] = row[i] - lower[k, i] * row[k]
        solved = row[7]
        for i in range(7):
            solved = jnp.where(sub == i, row[i], solved)
        change = rank8_product(now, solved)
        after = None
        if first + 8 < size:
            after = a_ref[first + 8 : first + 16, :]
            terms = [column(after, first + i) * row[i] for i in range(8)]
            while len(terms) > 1:
                terms = [terms[q] + terms[q + 1] for q in range(0, len(terms), 2)]
            after = jnp.where(here, 0.0, after) - terms[0]
        for q in range(0, size, 8):
            if q == first:
                a_ref[q : q + 8, :] = solved
            elif q == first + 8:
                a_ref[q : q + 8, :] = after
            else:
                old = jnp.where(here, 0.0, a_ref[q : q + 8, :])
                a_ref[q : q + 8, :] = old - change[q : q + 8, :]
        now = after


PIECES = (
    (slice(0, 128), slice(0, 128)),
    (slice(0, 128), slice(128, 256)),
    (slice(128, 256), slice(128, 256)),
    (slice(0, 256), slice(256, 384)),
)


def partner_of(level):
    dev, grp = lax.axis_index("dev"), lax.axis_index("grp")
    core, x, z = dev % 2, (dev // 2) % 4, dev // 8
    one = lambda flag, yes, no: jnp.where(flag, yes, no)
    new_core = one(level == 1, 1 - core, core)
    flip_x = x + 1 - 2 * (x % 2)
    new_x = one(level == 2, flip_x, one(level == 3, 3 - x, x))
    flip_z0 = z + 1 - 2 * (z % 2)
    flip_z1 = z + 2 - 4 * ((z // 2) % 2)
    new_z = one(level == 4, flip_z0, one(level == 5, flip_z1, one(level == 6, 7 - z, z)))
    flip_y = grp + 1 - 2 * (grp % 2)
    new_y = one(level == 7, flip_y, one(level == 8, 3 - grp, grp))
    return (new_y, (new_z * 4 + new_x) * 2 + new_core)


def kernel(
    inverse_hbm, basis_hbm, block_hbm, link_hbm, loads_hbm, order_ref, out_hbm,
    inverse, basis, block, link, loads, hot, leaf_w, leaf_y, lift, received, gain, part, value, low, high, result,
    in_sem, send_sem, recv_sem, out_sem,
):
    loaded = []
    for i, (src, dst) in enumerate(
        [(basis_hbm, basis), (inverse_hbm, inverse), (loads_hbm, loads), (block_hbm, block), (link_hbm, link)]
    ):
        loaded.append(pltpu.make_async_copy(src, dst, in_sem.at[i]))
        loaded[-1].start()
    barrier = pltpu.get_barrier_semaphore()
    for level in range(1, LEVELS + 1):
        pl.semaphore_signal(barrier, inc=1, device_id=partner_of(level), device_id_type=MESH)

    def exchange(level, piece):
        rows, columns = PIECES[piece]
        return pltpu.make_async_remote_copy(
            src_ref=lift.at[rows, columns],
            dst_ref=received.at[level - 1, rows, columns],
            send_sem=send_sem.at[level - 1, piece],
            recv_sem=recv_sem.at[level - 1, piece],
            device_id=partner_of(level),
            device_id_type=MESH,
        )

    loaded[0].wait()
    loaded[1].wait()
    leaf_w[...] = dot(inverse[...], basis[...])
    for piece in range(3):
        rows, columns = PIECES[piece]
        lift[rows, columns] = dot_tn(basis[:, rows], leaf_w[:, columns])
        if piece == 0:
            pl.semaphore_wait(barrier, LEVELS)
        exchange(1, piece).start()
    for copy in loaded[2:]:
        copy.wait()

    def leaf_loads():
        rows = lax.broadcasted_iota(jnp.int32, (LEAF, LEAF), 0)
        hot[...] = jnp.where(rows == order_ref[...], 1.0, 0.0).astype(BF)
        stacked = jnp.concatenate([p.astype(BF) for p in parts_of(loads[...])], axis=1)
        picked = dot_tn_exact(hot[...], stacked)
        leaf_y[...] = dot(inverse[...], whole(picked))
        lift[:, RANK:] = dot_tn(basis[...], leaf_y[...])
        exchange(1, 3).start()

    def to_initial_order():
        stacked = jnp.concatenate([p.astype(BF) for p in parts_of(leaf_y[...])], axis=1)
        leaf_y[...] = whole(jnp.dot(hot[...], stacked, preferred_element_type=F32))
        stacked = jnp.concatenate([p.astype(BF) for p in parts_of(leaf_w[...])], axis=1)
        leaf_w[...] = whole(jnp.dot(hot[...], stacked, preferred_element_type=F32))

    def node(level, carry):
        slot = level - 1
        base = slot * RANK
        top = pl.ds(pl.multiple_of(base, RANK), HALF)
        bottom = pl.ds(pl.multiple_of(base + HALF, HALF), HALF)

        def joined(rows, columns):
            return lift[rows, columns] + received[slot, rows, columns]

        exchange(level, 0).wait_recv()
        low[...] = block[top, 0:HALF] + joined(*PIECES[0])
        sweep(low)
        exchange(level, 1).wait_recv()
        exchange(level, 2).wait_recv()
        first = -low[...]
        cross = block[top, HALF:RANK] + joined(*PIECES[1])
        through = dot(first, cross)
        high[...] = block[bottom, HALF:RANK] + joined(*PIECES[2]) - dot_tn(cross, through)
        link_low = link[top, :]
        solved_low = dot(first, link_low)
        rest = link[bottom, :] - dot_tn(cross, solved_low)
        lifted = [
            dot_tn(link_low[:, rows], solved_low[:, columns]) for rows, columns in PIECES[:3]
        ]
        sweep(high)
        second = -high[...]
        solved_high = dot(second, rest)
        for piece in range(3):
            rows, columns = PIECES[piece]
            lifted[piece] += dot_tn(rest[:, rows], solved_high[:, columns])
            exchange(level, piece).wait_send()
            lift[rows, columns] = lifted[piece]

            @pl.when(level < LEVELS)
            def _():
                exchange(level + 1, piece).start()

        gain[slot, 0:HALF, :] = solved_low - dot(through, solved_high)
        gain[slot, HALF:RANK, :] = solved_high
        pl.when(level == 1)(leaf_loads)
        pl.when(level == 2)(to_initial_order)
        exchange(level, 3).wait_recv()
        sign = 2.0 * (level % 2).astype(F32) - 1.0
        target = sign * joined(*PIECES[3])
        part_low = dot(first, target[:HALF])
        part_rest = target[HALF:] - dot_tn(cross, part_low)
        part_high = dot(second, part_rest)
        exchange(level, 3).wait_send()
        lift[:, RANK:] = dot_tn(link_low, part_low) + dot_tn(rest, part_high)

        @pl.when(level < LEVELS)
        def _():
            exchange(level + 1, 3).start()

        part[slot, 0:HALF, :] = part_low - dot(through, part_high)
        part[slot, HALF:RANK, :] = part_high
        return carry

    lax.fori_loop(1, LEVELS + 1, node, 0)

    value[...] = part[LEVELS - 1]

    def down(step, carry):
        level = LEVELS - 1 - step
        sign = 1.0 - 2.0 * (level % 2).astype(F32)
        value[...] = part[level - 1] - sign * dot(gain[level - 1], value[...])
        return carry

    lax.fori_loop(0, LEVELS - 1, down, 0)
    result[...] = leaf_y[...] - dot(leaf_w[...], value[...])
    done = pltpu.make_async_copy(result, out_hbm, out_sem)
    done.start()
    done.wait()


def shards(leaf_inverse, leaf_basis, node_block, node_link, loads, order):
    hbm = pl.BlockSpec(memory_space=pltpu.HBM)
    return pl.pallas_call(
        kernel,
        out_shape=jax.ShapeDtypeStruct(loads.shape, F32),
        in_specs=[hbm] * 5 + [pl.BlockSpec(memory_space=pltpu.VMEM)],
        out_specs=hbm,
        scratch_shapes=[
            pltpu.VMEM((LEAF, LEAF), F32),
            pltpu.VMEM((LEAF, RANK), F32),
            pltpu.VMEM((LEVELS * RANK, RANK), F32),
            pltpu.VMEM((LEVELS * RANK, RANK), F32),
            pltpu.VMEM((LEAF, NRHS), F32),
            pltpu.VMEM((LEAF, LEAF), BF),
            pltpu.VMEM((LEAF, RANK), F32),
            pltpu.VMEM((LEAF, NRHS), F32),
            pltpu.VMEM((RANK, WIDE), F32),
            pltpu.VMEM((LEVELS, RANK, WIDE), F32),
            pltpu.VMEM((LEVELS, RANK, RANK), F32),
            pltpu.VMEM((LEVELS, RANK, NRHS), F32),
            pltpu.VMEM((RANK, NRHS), F32),
            pltpu.VMEM((HALF, HALF), F32),
            pltpu.VMEM((HALF, HALF), F32),
            pltpu.VMEM((LEAF, NRHS), F32),
            pltpu.SemaphoreType.DMA((5,)),
            pltpu.SemaphoreType.DMA((LEVELS, 4)),
            pltpu.SemaphoreType.DMA((LEVELS, 4)),
            pltpu.SemaphoreType.DMA,
        ],
        compiler_params=pltpu.CompilerParams(
            collective_id=0, has_side_effects=True, vmem_limit_bytes=63 * 1024 * 1024
        ),
        cost_estimate=pl.CostEstimate(flops=4_000_000_000, bytes_accessed=8_000_000, transcendentals=0),
    )(leaf_inverse, leaf_basis, node_block, node_link, loads, order)


def solution(mesh):
    spec = P(("grp", "dev"), None)
    return jax.shard_map(shards, mesh=mesh, in_specs=(spec,) * 6, out_specs=spec, check_vma=False)
```

```python
import functools
import jax
import jax.numpy as jnp
from jax import lax
from jax.experimental import pallas as pl
from jax.experimental.pallas import tpu as pltpu
from jax.sharding import PartitionSpec as P

BF = jnp.bfloat16
F32 = jnp.float32
MESH = pl.DeviceIdType.MESH
HALF = 128
RANK = 256
NRHS = 128
LEAF = 768
LEVELS = 8
AHEAD = 3
WIDE = RANK + NRHS
TERMS = ((0, 0), (0, 1), (1, 0), (0, 2), (2, 0), (1, 1))


def halves(x):
    high = x.astype(BF)
    return high, (x - high.astype(F32)).astype(BF)


def dot(a, b):
    ah, al = halves(a)
    bh, bl = halves(b)
    one = lambda p, q: jnp.dot(p, q, preferred_element_type=F32)
    return one(ah, bh) + (one(ah, bl) + one(al, bh))


def dot_tn(a, b):
    ah, al = halves(a)
    bh, bl = halves(b)
    one = lambda p, q: lax.dot_general(p, q, (((0,), (0,)), ((), ())), preferred_element_type=F32)
    return one(ah, bh) + (one(ah, bl) + one(al, bh))


def dot_tn_exact(a, b):
    return lax.dot_general(a, b, (((0,), (0,)), ((), ())), preferred_element_type=F32)


def whole(x):
    size = x.shape[1] // 3
    return (x[:, :size] + x[:, size : 2 * size]) + x[:, 2 * size :]


def parts_of(x):
    high = x.astype(BF).astype(F32)
    rest = x - high
    mid = rest.astype(BF).astype(F32)
    return (high, mid, rest - mid)


def rank8_product(rows, solved):
    a, b = parts_of(rows), parts_of(solved)
    left = jnp.concatenate([a[i] for i, _ in TERMS], axis=0).astype(BF)
    right = jnp.concatenate([b[j] for _, j in TERMS], axis=0).astype(BF)
    return lax.dot_general(left, right, (((0,), (0,)), ((), ())), preferred_element_type=F32)


def sweep(a_ref):
    size = a_ref.shape[0]
    groups = size // 8
    tile = (8, size)
    lane = lax.broadcasted_iota(jnp.int32, tile, 1)
    sub = lax.broadcasted_iota(jnp.int32, tile, 0)

    def spread(v, i):
        return jnp.broadcast_to(v[i : i + 1, :], tile)

    def column(v, j):
        return jnp.take_along_axis(v, jnp.full(tile, j, jnp.int32), axis=1)

    near = {g: a_ref[8 * g : 8 * g + 8, :] for g in range(AHEAD + 1)}
    diag = [column(near[0], j) for j in range(8)]
    cross = [column(near[1], j) for j in range(8)]
    for step in range(groups):
        first = 8 * step
        now = near.pop(step)
        here = (lane >= first) & (lane < first + 8)
        more = step + 1 < groups
        entry = {(i, j): spread(diag[j], i) for j in range(8) for i in range(j, 8)}
        row = [
            jnp.where(here, jnp.where(lane == first + i, -1.0, 0.0), spread(now, i))
            for i in range(8)
        ]
        if more:
            diag = [column(near[step + 1], first + 8 + j) for j in range(8)]
            reduced = list(cross)
        lower, pivot = {}, []
        for k in range(8):
            pivot.append(1.0 / entry[k, k])
            for i in range(k + 1, 8):
                lower[i, k] = entry[i, k] * pivot[k]
                for j in range(k + 1, i + 1):
                    entry[i, j] = entry[i, j] - lower[i, k] * entry[j, k]
                if more:
                    reduced[i] = reduced[i] - lower[i, k] * reduced[k]
            for i in range(k + 1, 8):
                row[i] = row[i] - lower[i, k] * row[k]
            if more:
                scaled = reduced[k] * pivot[k]
                diag = [diag[j] - scaled * spread(reduced[k], j) for j in range(8)]
        row = [r * p for r, p in zip(row, pivot)]
        for k in range(7, -1, -1):
            for i in range(k):
                row[i] = row[i] - lower[k, i] * row[k]
        solved = row[7]
        for i in range(7):
            solved = jnp.where(sub == i, row[i], solved)
        change = rank8_product(now, solved)
        later = {}
        for g in range(step + 1, min(groups, step + AHEAD + 1)):
            old = near[g] if g in near else a_ref[8 * g : 8 * g + 8, :]
            columns = cross if g == step + 1 else [column(old, first + i) for i in range(8)]
            terms = [c * r for c, r in zip(columns, row)]
            while len(terms) > 1:
                terms = [terms[q] + terms[q + 1] for q in range(0, len(terms), 2)]
            later[g] = jnp.where(here, 0.0, old) - terms[0]
        for g in range(groups):
            rows = slice(8 * g, 8 * g + 8)
            if g == step:
                a_ref[rows, :] = solved
            elif g not in later:
                a_ref[rows, :] = jnp.where(here, 0.0, a_ref[rows, :]) - change[rows, :]
        near = later
        if step + 2 < groups:
            cross = [column(near[step + 2], first + 8 + i) for i in range(8)]


PIECES = (
    (slice(0, 128), slice(0, 128)),
    (slice(0, 128), slice(128, 256)),
    (slice(128, 256), slice(128, 256)),
    (slice(0, 256), slice(256, 384)),
)


def partner_of(level):
    dev, grp = lax.axis_index("dev"), lax.axis_index("grp")
    core, x, z = dev % 2, (dev // 2) % 4, dev // 8
    one = lambda flag, yes, no: jnp.where(flag, yes, no)
    new_core = one(level == 1, 1 - core, core)
    flip_x = x + 1 - 2 * (x % 2)
    new_x = one(level == 2, flip_x, one(level == 3, 3 - x, x))
    flip_z0 = z + 1 - 2 * (z % 2)
    flip_z1 = z + 2 - 4 * ((z // 2) % 2)
    new_z = one(level == 4, flip_z0, one(level == 5, flip_z1, one(level == 6, 7 - z, z)))
    flip_y = grp + 1 - 2 * (grp % 2)
    new_y = one(level == 7, flip_y, one(level == 8, 3 - grp, grp))
    return (new_y, (new_z * 4 + new_x) * 2 + new_core)


def kernel(
    inverse_hbm, basis_hbm, block_hbm, link_hbm, loads_hbm, order_ref, out_hbm,
    inverse, basis, block, link, loads, hot, leaf_w, leaf_y, lift, received, gain, part, value, low, high, result,
    in_sem, send_sem, recv_sem, out_sem,
):
    loaded = []
    for i, (src, dst) in enumerate(
        [(basis_hbm, basis), (inverse_hbm, inverse), (loads_hbm, loads), (block_hbm, block), (link_hbm, link)]
    ):
        loaded.append(pltpu.make_async_copy(src, dst, in_sem.at[i]))
        loaded[-1].start()
    barrier = pltpu.get_barrier_semaphore()
    for level in range(1, LEVELS + 1):
        pl.semaphore_signal(barrier, inc=1, device_id=partner_of(level), device_id_type=MESH)

    def exchange(level, piece):
        rows, columns = PIECES[piece]
        return pltpu.make_async_remote_copy(
            src_ref=lift.at[rows, columns],
            dst_ref=received.at[level - 1, rows, columns],
            send_sem=send_sem.at[level - 1, piece],
            recv_sem=recv_sem.at[level - 1, piece],
            device_id=partner_of(level),
            device_id_type=MESH,
        )

    core = lax.axis_index("dev") % 2
    mine = pl.ds(pl.multiple_of(core * HALF, HALF), HALF)
    sides = slice(RANK, WIDE)

    def exchange_half(level):
        return pltpu.make_async_remote_copy(
            src_ref=lift.at[mine, sides],
            dst_ref=received.at[level - 1, mine, sides],
            send_sem=send_sem.at[level - 1, 3],
            recv_sem=recv_sem.at[level - 1, 3],
            device_id=partner_of(level),
            device_id_type=MESH,
        )

    def relay_half(level):
        return pltpu.make_async_remote_copy(
            src_ref=received.at[level - 1, mine, sides],
            dst_ref=received.at[level - 1, mine, sides],
            send_sem=send_sem.at[level - 1, 4],
            recv_sem=recv_sem.at[level - 1, 4],
            device_id=partner_of(1),
            device_id_type=MESH,
        )

    loaded[0].wait()
    loaded[1].wait()
    leaf_w[...] = dot(inverse[...], basis[...])
    for piece in range(3):
        rows, columns = PIECES[piece]
        lift[rows, columns] = dot_tn(basis[:, rows], leaf_w[:, columns])
        if piece == 0:
            pl.semaphore_wait(barrier, LEVELS)
        exchange(1, piece).start()
    for copy in loaded[2:]:
        copy.wait()
    rows = lax.broadcasted_iota(jnp.int32, (LEAF, LEAF), 0)
    hot[...] = jnp.where(rows == order_ref[...], 1.0, 0.0).astype(BF)
    stacked = jnp.concatenate([p.astype(BF) for p in parts_of(loads[...])], axis=1)
    leaf_y[...] = whole(dot_tn_exact(hot[...], stacked))

    def leaf_loads():
        leaf_y[...] = dot(inverse[...], leaf_y[...])
        lift[:, RANK:] = dot_tn(basis[...], leaf_y[...])
        exchange(1, 3).start()

    def to_initial_order():
        stacked = jnp.concatenate([p.astype(BF) for p in parts_of(leaf_y[...])], axis=1)
        leaf_y[...] = whole(jnp.dot(hot[...], stacked, preferred_element_type=F32))
        stacked = jnp.concatenate([p.astype(BF) for p in parts_of(leaf_w[...])], axis=1)
        leaf_w[...] = whole(jnp.dot(hot[...], stacked, preferred_element_type=F32))

    def node(level, carry):
        slot = level - 1
        base = slot * RANK
        top = pl.ds(pl.multiple_of(base, RANK), HALF)
        bottom = pl.ds(pl.multiple_of(base + HALF, HALF), HALF)

        def joined(rows, columns):
            return lift[rows, columns] + received[slot, rows, columns]

        exchange(level, 0).wait_recv()
        low[...] = block[top, 0:HALF] + joined(*PIECES[0])
        sweep(low)
        exchange(level, 1).wait_recv()
        exchange(level, 2).wait_recv()
        first = -low[...]
        cross = block[top, HALF:RANK] + joined(*PIECES[1])
        through = dot(first, cross)
        high[...] = block[bottom, HALF:RANK] + joined(*PIECES[2]) - dot_tn(cross, through)
        link_low = link[top, :]
        solved_low = dot(first, link_low)
        rest = link[bottom, :] - dot_tn(cross, solved_low)
        lifted = [
            dot_tn(link_low[:, rows], solved_low[:, columns]) for rows, columns in PIECES[:3]
        ]
        sweep(high)
        second = -high[...]
        for piece in range(3):
            exchange(level, piece).wait_send()

        @pl.when(level < LEVELS)
        def _():
            solved_high = dot(second, rest)
            for piece in range(3):
                rows, columns = PIECES[piece]
                lift[rows, columns] = lifted[piece] + dot_tn(rest[:, rows], solved_high[:, columns])
                exchange(level + 1, piece).start()
            gain[slot, HALF:RANK, :] = solved_high

        pl.when(level == 1)(leaf_loads)

        @pl.when(level > 1)
        def _():
            exchange_half(level).wait_recv()
            relay_half(level).start()

        pl.when(level == 5)(to_initial_order)

        @pl.when(level < LEVELS)
        def _():
            gain[slot, 0:HALF, :] = solved_low - dot(through, gain[slot, HALF:RANK, :])

        @pl.when(level == 1)
        def _():
            exchange(1, 3).wait()

        @pl.when(level > 1)
        def _():
            relay_half(level).wait()
            exchange_half(level).wait_send()

        sign = 2.0 * (level % 2).astype(F32) - 1.0
        target = sign * joined(*PIECES[3])
        part_low = dot(first, target[:HALF])
        part_rest = target[HALF:] - dot_tn(cross, part_low)
        part_high = dot(second, part_rest)

        @pl.when(level < LEVELS)
        def _():
            lift[:, RANK:] = dot_tn(link_low, part_low) + dot_tn(rest, part_high)
            exchange_half(level + 1).start()

        part[slot, 0:HALF, :] = part_low - dot(through, part_high)
        part[slot, HALF:RANK, :] = part_high
        return carry

    lax.fori_loop(1, LEVELS + 1, node, 0)

    value[...] = part[LEVELS - 1]

    def down(step, carry):
        level = LEVELS - 1 - step
        sign = 1.0 - 2.0 * (level % 2).astype(F32)
        value[...] = part[level - 1] - sign * dot(gain[level - 1], value[...])
        return carry

    lax.fori_loop(0, LEVELS - 1, down, 0)
    result[...] = leaf_y[...] - dot(leaf_w[...], value[...])
    done = pltpu.make_async_copy(result, out_hbm, out_sem)
    done.start()
    done.wait()


def shards(leaf_inverse, leaf_basis, node_block, node_link, loads, order):
    hbm = pl.BlockSpec(memory_space=pltpu.HBM)
    return pl.pallas_call(
        kernel,
        out_shape=jax.ShapeDtypeStruct(loads.shape, F32),
        in_specs=[hbm] * 5 + [pl.BlockSpec(memory_space=pltpu.VMEM)],
        out_specs=hbm,
        scratch_shapes=[
            pltpu.VMEM((LEAF, LEAF), F32),
            pltpu.VMEM((LEAF, RANK), F32),
            pltpu.VMEM((LEVELS * RANK, RANK), F32),
            pltpu.VMEM((LEVELS * RANK, RANK), F32),
            pltpu.VMEM((LEAF, NRHS), F32),
            pltpu.VMEM((LEAF, LEAF), BF),
            pltpu.VMEM((LEAF, RANK), F32),
            pltpu.VMEM((LEAF, NRHS), F32),
            pltpu.VMEM((RANK, WIDE), F32),
            pltpu.VMEM((LEVELS, RANK, WIDE), F32),
            pltpu.VMEM((LEVELS, RANK, RANK), F32),
            pltpu.VMEM((LEVELS, RANK, NRHS), F32),
            pltpu.VMEM((RANK, NRHS), F32),
            pltpu.VMEM((HALF, HALF), F32),
            pltpu.VMEM((HALF, HALF), F32),
            pltpu.VMEM((LEAF, NRHS), F32),
            pltpu.SemaphoreType.DMA((5,)),
            pltpu.SemaphoreType.DMA((LEVELS, 5)),
            pltpu.SemaphoreType.DMA((LEVELS, 5)),
            pltpu.SemaphoreType.DMA,
        ],
        compiler_params=pltpu.CompilerParams(
            collective_id=0, has_side_effects=True, vmem_limit_bytes=63 * 1024 * 1024
        ),
        cost_estimate=pl.CostEstimate(flops=4_000_000_000, bytes_accessed=8_000_000, transcendentals=0),
    )(leaf_inverse, leaf_basis, node_block, node_link, loads, order)


def solution(mesh):
    spec = P(("grp", "dev"), None)
    return jax.shard_map(shards, mesh=mesh, in_specs=(spec,) * 6, out_specs=spec, check_vma=False)
```

```python
import functools
import jax
import jax.numpy as jnp
from jax import lax
from jax.experimental import pallas as pl
from jax.experimental.pallas import tpu as pltpu
from jax.sharding import PartitionSpec as P

BF = jnp.bfloat16
F32 = jnp.float32
MESH = pl.DeviceIdType.MESH
HALF = 128
RANK = 256
NRHS = 128
LEAF = 768
LEVELS = 8
AHEAD = 2
WIDE = RANK + NRHS
TERMS = ((0, 0), (0, 1), (1, 0), (0, 2), (2, 0), (1, 1))


def halves(x):
    high = x.astype(BF)
    return high, (x - high.astype(F32)).astype(BF)


def dot_parts(a, b):
    one = lambda p, q: jnp.dot(p, q, preferred_element_type=F32)
    return one(a[0], b[0]) + (one(a[0], b[1]) + one(a[1], b[0]))


def dot(a, b):
    return dot_parts(halves(a), halves(b))


def dot_tn(a, b):
    ah, al = halves(a)
    bh, bl = halves(b)
    one = lambda p, q: lax.dot_general(p, q, (((0,), (0,)), ((), ())), preferred_element_type=F32)
    return one(ah, bh) + (one(ah, bl) + one(al, bh))


def dot_tn_exact(a, b):
    return lax.dot_general(a, b, (((0,), (0,)), ((), ())), preferred_element_type=F32)


def whole(x):
    size = x.shape[1] // 3
    return (x[:, :size] + x[:, size : 2 * size]) + x[:, 2 * size :]


def parts_of(x):
    high = x.astype(BF).astype(F32)
    rest = x - high
    mid = rest.astype(BF).astype(F32)
    return (high, mid, rest - mid)


def rank_product(rows, solved):
    a, b = parts_of(rows), parts_of(solved)
    left = jnp.concatenate([a[i] for i, _ in TERMS], axis=0).astype(BF)
    right = jnp.concatenate([b[j] for _, j in TERMS], axis=0).astype(BF)
    return lax.dot_general(left, right, (((0,), (0,)), ((), ())), preferred_element_type=F32)


def sweep(a_ref):
    size = a_ref.shape[0]
    groups = size // 8
    tile = (8, size)
    lane = lax.broadcasted_iota(jnp.int32, tile, 1)
    sub = lax.broadcasted_iota(jnp.int32, tile, 0)

    def spread(v, i):
        return jnp.broadcast_to(v[i : i + 1, :], tile)

    def column(v, j):
        return jnp.take_along_axis(v, jnp.full(tile, j, jnp.int32), axis=1)

    def updated(old, first, row, columns=None):
        columns = columns or [column(old, first + i) for i in range(8)]
        terms = [c * r for c, r in zip(columns, row)]
        while len(terms) > 1:
            terms = [terms[q] + terms[q + 1] for q in range(0, len(terms), 2)]
        here = (lane >= first) & (lane < first + 8)
        return jnp.where(here, 0.0, old) - terms[0]

    near = {g: a_ref[8 * g : 8 * g + 8, :] for g in range(AHEAD + 1)}
    diag = [column(near[0], j) for j in range(8)]
    cross = [column(near[1], j) for j in range(8)]
    lefts, rights, swept = [], [], {}
    for step in range(groups):
        first = 8 * step
        now = near.pop(step)
        here = (lane >= first) & (lane < first + 8)
        more = step + 1 < groups
        entry = {(i, j): spread(diag[j], i) for j in range(8) for i in range(j, 8)}
        row = [
            jnp.where(here, jnp.where(lane == first + i, -1.0, 0.0), spread(now, i))
            for i in range(8)
        ]
        if more:
            diag = [column(near[step + 1], first + 8 + j) for j in range(8)]
            reduced = list(cross)
        lower, pivot = {}, []
        for k in range(8):
            pivot.append(1.0 / entry[k, k])
            for i in range(k + 1, 8):
                lower[i, k] = entry[i, k] * pivot[k]
                for j in range(k + 1, i + 1):
                    entry[i, j] = entry[i, j] - lower[i, k] * entry[j, k]
                if more:
                    reduced[i] = reduced[i] - lower[i, k] * reduced[k]
            for i in range(k + 1, 8):
                row[i] = row[i] - lower[i, k] * row[k]
            if more:
                scaled = reduced[k] * pivot[k]
                diag = [diag[j] - scaled * spread(reduced[k], j) for j in range(8)]
        row = [r * p for r, p in zip(row, pivot)]
        for k in range(7, -1, -1):
            for i in range(k):
                row[i] = row[i] - lower[k, i] * row[k]
        solved = row[7]
        for i in range(7):
            solved = jnp.where(sub == i, row[i], solved)
        reach = step + AHEAD + (1 - step % 2)
        later = {}
        for g in range(step + 1, min(groups, reach + 1)):
            old = near[g] if g in near else a_ref[8 * g : 8 * g + 8, :]
            later[g] = updated(old, first, row, cross if g == step + 1 else None)
        swept = {g: updated(old, first, row) for g, old in swept.items()}
        swept[step] = solved
        lefts.append(now)
        rights = [jnp.where(here, 0.0, r) for r in rights] + [solved]
        if step % 2:
            change = rank_product(jnp.concatenate(lefts, axis=0), jnp.concatenate(rights, axis=0))
            gone = (lane >= first - 8) & (lane < first + 8)
            for g in range(groups):
                rows = slice(8 * g, 8 * g + 8)
                if g in swept:
                    a_ref[rows, :] = swept[g]
                elif g not in later:
                    a_ref[rows, :] = jnp.where(gone, 0.0, a_ref[rows, :]) - change[rows, :]
            lefts, rights, swept = [], [], {}
        near = later
        if step + 2 < groups:
            cross = [column(near[step + 2], first + 8 + i) for i in range(8)]


PIECES = (
    (slice(0, 128), slice(0, 128)),
    (slice(0, 128), slice(128, 256)),
    (slice(128, 256), slice(128, 256)),
    (slice(0, 256), slice(256, 384)),
)


def partner_of(level):
    dev, grp = lax.axis_index("dev"), lax.axis_index("grp")
    core, x, z = dev % 2, (dev // 2) % 4, dev // 8
    one = lambda flag, yes, no: jnp.where(flag, yes, no)
    new_core = one(level == 1, 1 - core, core)
    flip_x = x + 1 - 2 * (x % 2)
    new_x = one(level == 2, flip_x, one(level == 3, 3 - x, x))
    flip_z0 = z + 1 - 2 * (z % 2)
    flip_z1 = z + 2 - 4 * ((z // 2) % 2)
    new_z = one(level == 4, flip_z0, one(level == 5, flip_z1, one(level == 6, 7 - z, z)))
    flip_y = grp + 1 - 2 * (grp % 2)
    new_y = one(level == 7, flip_y, one(level == 8, 3 - grp, grp))
    return (new_y, (new_z * 4 + new_x) * 2 + new_core)


def kernel(
    inverse_hbm, basis_hbm, block_hbm, link_hbm, loads_hbm, order_ref, out_hbm,
    inverse, basis, block, link, loads, hot, leaf_w, leaf_y, lift, received, gain, part, value, low, high, result,
    in_sem, send_sem, recv_sem, out_sem,
):
    loaded = []
    for i, (src, dst) in enumerate(
        [(basis_hbm, basis), (inverse_hbm, inverse), (loads_hbm, loads), (block_hbm, block), (link_hbm, link)]
    ):
        loaded.append(pltpu.make_async_copy(src, dst, in_sem.at[i]))
        loaded[-1].start()
    barrier = pltpu.get_barrier_semaphore()
    for level in range(1, LEVELS + 1):
        pl.semaphore_signal(barrier, inc=1, device_id=partner_of(level), device_id_type=MESH)

    def exchange(level, piece):
        rows, columns = PIECES[piece]
        return pltpu.make_async_remote_copy(
            src_ref=lift.at[rows, columns],
            dst_ref=received.at[level - 1, rows, columns],
            send_sem=send_sem.at[level - 1, piece],
            recv_sem=recv_sem.at[level - 1, piece],
            device_id=partner_of(level),
            device_id_type=MESH,
        )

    core = lax.axis_index("dev") % 2
    mine = pl.ds(pl.multiple_of(core * HALF, HALF), HALF)
    sides, outer = slice(RANK, WIDE), slice(HALF, RANK)

    def crowded(level):
        return (level - 5) * (level - 6) == 0

    def roomy(level):
        return (level - 5) * (level - 6) != 0


    def exchange_half(level, columns, slot):
        return pltpu.make_async_remote_copy(
            src_ref=lift.at[mine, columns],
            dst_ref=received.at[level - 1, mine, columns],
            send_sem=send_sem.at[level - 1, slot],
            recv_sem=recv_sem.at[level - 1, slot],
            device_id=partner_of(level),
            device_id_type=MESH,
        )

    def relay_half(level, columns, slot):
        return pltpu.make_async_remote_copy(
            src_ref=received.at[level - 1, mine, columns],
            dst_ref=received.at[level - 1, mine, columns],
            send_sem=send_sem.at[level - 1, slot],
            recv_sem=recv_sem.at[level - 1, slot],
            device_id=partner_of(1),
            device_id_type=MESH,
        )

    loaded[0].wait()
    loaded[1].wait()
    leaf_w[...] = dot(inverse[...], basis[...])
    for piece in range(3):
        rows, columns = PIECES[piece]
        lift[rows, columns] = dot_tn(basis[:, rows], leaf_w[:, columns])
        if piece == 0:
            pl.semaphore_wait(barrier, LEVELS)
        exchange(1, piece).start()
    for copy in loaded[2:]:
        copy.wait()
    rows = lax.broadcasted_iota(jnp.int32, (LEAF, LEAF), 0)
    hot[...] = jnp.where(rows == order_ref[...], 1.0, 0.0).astype(BF)
    stacked = jnp.concatenate([p.astype(BF) for p in parts_of(loads[...])], axis=1)
    leaf_y[...] = whole(dot_tn_exact(hot[...], stacked))

    def leaf_loads():
        leaf_y[...] = dot(inverse[...], leaf_y[...])
        lift[:, RANK:] = dot_tn(basis[...], leaf_y[...])
        exchange(1, 3).start()

    def to_initial_order():
        stacked = jnp.concatenate([p.astype(BF) for p in parts_of(leaf_y[...])], axis=1)
        leaf_y[...] = whole(jnp.dot(hot[...], stacked, preferred_element_type=F32))
        stacked = jnp.concatenate([p.astype(BF) for p in parts_of(leaf_w[...])], axis=1)
        leaf_w[...] = whole(jnp.dot(hot[...], stacked, preferred_element_type=F32))

    def node(level, carry):
        slot = level - 1
        base = slot * RANK
        top = pl.ds(pl.multiple_of(base, RANK), HALF)
        bottom = pl.ds(pl.multiple_of(base + HALF, HALF), HALF)

        def joined(rows, columns):
            return lift[rows, columns] + received[slot, rows, columns]

        exchange(level, 0).wait_recv()
        low[...] = block[top, 0:HALF] + joined(*PIECES[0])
        sweep(low)

        @pl.when(roomy(level))
        def _():
            exchange(level, 1).wait_recv()
            exchange(level, 2).wait_recv()

        @pl.when(crowded(level))
        def _():
            exchange_half(level, outer, 1).wait_recv()
            relay_half(level, outer, 2).start()
            relay_half(level, outer, 2).wait()

        first = -low[...]
        cross = block[top, HALF:RANK] + joined(*PIECES[1])
        through = dot(first, cross)
        high[...] = block[bottom, HALF:RANK] + joined(*PIECES[2]) - dot_tn(cross, through)
        link_low = link[top, :]
        solved_low = dot(first, link_low)
        rest = link[bottom, :] - dot_tn(cross, solved_low)
        lifted = [
            dot_tn(link_low[:, rows], solved_low[:, columns]) for rows, columns in PIECES[:3]
        ]
        rest_parts, turned_parts = halves(rest), halves(rest.T)
        sweep(high)
        second = -high[...]
        exchange(level, 0).wait_send()

        @pl.when(roomy(level))
        def _():
            exchange(level, 1).wait_send()
            exchange(level, 2).wait_send()

        @pl.when(crowded(level))
        def _():
            exchange_half(level, outer, 1).wait_send()
            exchange_half(level, sides, 3).wait_recv()
            relay_half(level, sides, 4).start()

        @pl.when(level < LEVELS)
        def _():
            inverse_parts = halves(second)
            near = dot_parts(inverse_parts, [p[:, :HALF] for p in rest_parts])
            near_parts = halves(near)
            lift[0:HALF, 0:HALF] = lifted[0] + dot_parts([p[:HALF] for p in turned_parts], near_parts)
            exchange(level + 1, 0).start()
            far = dot_parts(inverse_parts, [p[:, HALF:] for p in rest_parts])
            both = dot_parts(turned_parts, halves(far))
            lift[0:HALF, HALF:RANK] = lifted[1] + both[:HALF]
            lift[HALF:RANK, HALF:RANK] = lifted[2] + both[HALF:]

            @pl.when(roomy(level + 1))
            def _():
                exchange(level + 1, 1).start()
                exchange(level + 1, 2).start()

            @pl.when(crowded(level + 1))
            def _():
                exchange_half(level + 1, outer, 1).start()

            gain[slot, HALF:RANK, 0:HALF] = near
            gain[slot, HALF:RANK, HALF:RANK] = far

        pl.when(level == 1)(leaf_loads)

        pl.when(level == 5)(to_initial_order)

        @pl.when(level < LEVELS)
        def _():
            gain[slot, 0:HALF, :] = solved_low - dot(through, gain[slot, HALF:RANK, :])

        @pl.when(roomy(level))
        def _():
            exchange(level, 3).wait()

        @pl.when(crowded(level))
        def _():
            relay_half(level, sides, 4).wait()
            exchange_half(level, sides, 3).wait_send()

        sign = 2.0 * (level % 2).astype(F32) - 1.0
        target = sign * joined(*PIECES[3])
        part_low = dot(first, target[:HALF])
        part_rest = target[HALF:] - dot_tn(cross, part_low)
        part_high = dot(second, part_rest)

        @pl.when(level < LEVELS)
        def _():
            lift[:, RANK:] = dot_tn(link_low, part_low) + dot_tn(rest, part_high)

            @pl.when(roomy(level + 1))
            def _():
                exchange(level + 1, 3).start()

            @pl.when(crowded(level + 1))
            def _():
                exchange_half(level + 1, sides, 3).start()

        part[slot, 0:HALF, :] = part_low - dot(through, part_high)
        part[slot, HALF:RANK, :] = part_high
        return carry

    lax.fori_loop(1, LEVELS + 1, node, 0)

    value[...] = part[LEVELS - 1]

    def down(step, carry):
        level = LEVELS - 1 - step
        sign = 1.0 - 2.0 * (level % 2).astype(F32)
        value[...] = part[level - 1] - sign * dot(gain[level - 1], value[...])
        return carry

    lax.fori_loop(0, LEVELS - 1, down, 0)
    result[...] = leaf_y[...] - dot(leaf_w[...], value[...])
    done = pltpu.make_async_copy(result, out_hbm, out_sem)
    done.start()
    done.wait()


def shards(leaf_inverse, leaf_basis, node_block, node_link, loads, order):
    hbm = pl.BlockSpec(memory_space=pltpu.HBM)
    return pl.pallas_call(
        kernel,
        out_shape=jax.ShapeDtypeStruct(loads.shape, F32),
        in_specs=[hbm] * 5 + [pl.BlockSpec(memory_space=pltpu.VMEM)],
        out_specs=hbm,
        scratch_shapes=[
            pltpu.VMEM((LEAF, LEAF), F32),
            pltpu.VMEM((LEAF, RANK), F32),
            pltpu.VMEM((LEVELS * RANK, RANK), F32),
            pltpu.VMEM((LEVELS * RANK, RANK), F32),
            pltpu.VMEM((LEAF, NRHS), F32),
            pltpu.VMEM((LEAF, LEAF), BF),
            pltpu.VMEM((LEAF, RANK), F32),
            pltpu.VMEM((LEAF, NRHS), F32),
            pltpu.VMEM((RANK, WIDE), F32),
            pltpu.VMEM((LEVELS, RANK, WIDE), F32),
            pltpu.VMEM((LEVELS, RANK, RANK), F32),
            pltpu.VMEM((LEVELS, RANK, NRHS), F32),
            pltpu.VMEM((RANK, NRHS), F32),
            pltpu.VMEM((HALF, HALF), F32),
            pltpu.VMEM((HALF, HALF), F32),
            pltpu.VMEM((LEAF, NRHS), F32),
            pltpu.SemaphoreType.DMA((5,)),
            pltpu.SemaphoreType.DMA((LEVELS, 5)),
            pltpu.SemaphoreType.DMA((LEVELS, 5)),
            pltpu.SemaphoreType.DMA,
        ],
        compiler_params=pltpu.CompilerParams(
            collective_id=0, has_side_effects=True, vmem_limit_bytes=63 * 1024 * 1024
        ),
        cost_estimate=pl.CostEstimate(flops=4_000_000_000, bytes_accessed=8_000_000, transcendentals=0),
    )(leaf_inverse, leaf_basis, node_block, node_link, loads, order)


def solution(mesh):
    spec = P(("grp", "dev"), None)
    return jax.shard_map(shards, mesh=mesh, in_specs=(spec,) * 6, out_specs=spec, check_vma=False)
```

```python
import functools
import jax
import jax.numpy as jnp
from jax import lax
from jax.experimental import pallas as pl
from jax.experimental.pallas import tpu as pltpu
from jax.sharding import PartitionSpec as P

BF = jnp.bfloat16
F32 = jnp.float32
MESH = pl.DeviceIdType.MESH
HALF = 128
RANK = 256
NRHS = 128
LEAF = 768
LEVELS = 8
AHEAD = 2
LATE = 48
WIDE = RANK + NRHS
TERMS = ((0, 0), (0, 1), (1, 0), (0, 2), (2, 0), (1, 1))


def halves(x):
    high = x.astype(BF)
    return high, (x - high.astype(F32)).astype(BF)


def dot_parts(a, b):
    one = lambda p, q: jnp.dot(p, q, preferred_element_type=F32)
    return one(a[0], b[0]) + (one(a[0], b[1]) + one(a[1], b[0]))


def dot(a, b):
    return dot_parts(halves(a), halves(b))


def dot_tn(a, b):
    ah, al = halves(a)
    bh, bl = halves(b)
    one = lambda p, q: lax.dot_general(p, q, (((0,), (0,)), ((), ())), preferred_element_type=F32)
    return one(ah, bh) + (one(ah, bl) + one(al, bh))


def dot_tn_exact(a, b):
    return lax.dot_general(a, b, (((0,), (0,)), ((), ())), preferred_element_type=F32)


def whole(x):
    size = x.shape[1] // 3
    return (x[:, :size] + x[:, size : 2 * size]) + x[:, 2 * size :]


def parts_of(x):
    high = x.astype(BF).astype(F32)
    rest = x - high
    mid = rest.astype(BF).astype(F32)
    return (high, mid, rest - mid)


def rank_product(rows, solved):
    a, b = parts_of(rows), parts_of(solved)
    left = jnp.concatenate([a[i] for i, _ in TERMS], axis=0).astype(BF)
    right = jnp.concatenate([b[j] for _, j in TERMS], axis=0).astype(BF)
    return lax.dot_general(left, right, (((0,), (0,)), ((), ())), preferred_element_type=F32)


def sweep(a_ref, late=None):
    size = a_ref.shape[0]
    groups = size // 8
    tile = (8, size)
    lane = lax.broadcasted_iota(jnp.int32, tile, 1)
    sub = lax.broadcasted_iota(jnp.int32, tile, 0)

    def spread(v, i):
        return jnp.broadcast_to(v[i : i + 1, :], tile)

    def column(v, j):
        return jnp.take_along_axis(v, jnp.full(tile, j, jnp.int32), axis=1)

    def updated(old, first, row, columns=None):
        columns = columns or [column(old, first + i) for i in range(8)]
        terms = [c * r for c, r in zip(columns, row)]
        while len(terms) > 1:
            terms = [terms[q] + terms[q + 1] for q in range(0, len(terms), 2)]
        here = (lane >= first) & (lane < first + 8)
        return jnp.where(here, 0.0, old) - terms[0]

    near = {g: a_ref[8 * g : 8 * g + 8, :] for g in range(AHEAD + 1)}
    diag = [column(near[0], j) for j in range(8)]
    cross = [column(near[1], j) for j in range(8)]
    lefts, rights, swept = [], [], {}
    for step in range(groups):
        first = 8 * step
        now = near.pop(step)
        here = (lane >= first) & (lane < first + 8)
        more = step + 1 < groups
        entry = {(i, j): spread(diag[j], i) for j in range(8) for i in range(j, 8)}
        row = [
            jnp.where(here, jnp.where(lane == first + i, -1.0, 0.0), spread(now, i))
            for i in range(8)
        ]
        if more:
            diag = [column(near[step + 1], first + 8 + j) for j in range(8)]
            reduced = list(cross)
        lower, pivot = {}, []
        for k in range(8):
            pivot.append(1.0 / entry[k, k])
            for i in range(k + 1, 8):
                lower[i, k] = entry[i, k] * pivot[k]
                for j in range(k + 1, i + 1):
                    entry[i, j] = entry[i, j] - lower[i, k] * entry[j, k]
                if more:
                    reduced[i] = reduced[i] - lower[i, k] * reduced[k]
            for i in range(k + 1, 8):
                row[i] = row[i] - lower[i, k] * row[k]
            if more:
                scaled = reduced[k] * pivot[k]
                diag = [diag[j] - scaled * spread(reduced[k], j) for j in range(8)]
        row = [r * p for r, p in zip(row, pivot)]
        for k in range(7, -1, -1):
            for i in range(k):
                row[i] = row[i] - lower[k, i] * row[k]
        solved = row[7]
        for i in range(7):
            solved = jnp.where(sub == i, row[i], solved)
        reach = step + AHEAD + (1 - step % 2)
        later = {}
        for g in range(step + 1, min(groups, reach + 1)):
            old = near[g] if g in near else a_ref[8 * g : 8 * g + 8, :]
            later[g] = updated(old, first, row, cross if g == step + 1 else None)
        swept = {g: updated(old, first, row) for g, old in swept.items()}
        swept[step] = solved
        lefts.append(now)
        rights = [jnp.where(here, 0.0, r) for r in rights] + [solved]
        if step % 2:
            change = rank_product(jnp.concatenate(lefts, axis=0), jnp.concatenate(rights, axis=0))
            gone = (lane >= first - 8) & (lane < first + 8)
            for g in range(groups):
                rows = slice(8 * g, 8 * g + 8)
                if g in swept:
                    a_ref[rows, :] = swept[g]
                elif g not in later:
                    a_ref[rows, :] = jnp.where(gone, 0.0, a_ref[rows, :]) - change[rows, :]
            lefts, rights, swept = [], [], {}
            if late is not None and first + 8 == LATE:
                late()
        near = later
        if step + 2 < groups:
            cross = [column(near[step + 2], first + 8 + i) for i in range(8)]


PIECES = (
    (slice(0, 64), slice(0, 128)),
    (slice(0, 128), slice(128, 256)),
    (slice(128, 256), slice(128, 256)),
    (slice(0, 256), slice(256, 384)),
    (slice(64, 128), slice(0, 128)),
)
BLOCKS = ((slice(0, 128), slice(0, 128)),) + PIECES[1:3]


def partner_of(level):
    dev, grp = lax.axis_index("dev"), lax.axis_index("grp")
    core, x, z = dev % 2, (dev // 2) % 4, dev // 8
    one = lambda flag, yes, no: jnp.where(flag, yes, no)
    new_core = one(level == 1, 1 - core, core)
    flip_x = x + 1 - 2 * (x % 2)
    new_x = one(level == 2, flip_x, one(level == 3, 3 - x, x))
    flip_z0 = z + 1 - 2 * (z % 2)
    flip_z1 = z + 2 - 4 * ((z // 2) % 2)
    new_z = one(level == 4, flip_z0, one(level == 5, flip_z1, one(level == 6, 7 - z, z)))
    flip_y = grp + 1 - 2 * (grp % 2)
    new_y = one(level == 7, flip_y, one(level == 8, 3 - grp, grp))
    return (new_y, (new_z * 4 + new_x) * 2 + new_core)


def kernel(
    inverse_hbm, basis_hbm, block_hbm, link_hbm, loads_hbm, order_ref, out_hbm,
    inverse, basis, block, link, loads, hot, leaf_w, leaf_y, lift, received, gain, part, value, low, high, result,
    in_sem, send_sem, recv_sem, out_sem,
):
    loaded = []
    bands = [pl.ds(RANK * i, RANK) for i in range(LEAF // RANK)]
    for i, (src, dst) in enumerate(
        [(basis_hbm, basis)]
        + [(inverse_hbm.at[band], inverse.at[band]) for band in bands]
        + [(loads_hbm, loads), (block_hbm, block), (link_hbm, link)]
    ):
        loaded.append(pltpu.make_async_copy(src, dst, in_sem.at[i]))
        loaded[-1].start()
    barrier = pltpu.get_barrier_semaphore()
    for level in range(1, LEVELS + 1):
        pl.semaphore_signal(barrier, inc=1, device_id=partner_of(level), device_id_type=MESH)

    def exchange(level, piece):
        rows, columns = PIECES[piece]
        return pltpu.make_async_remote_copy(
            src_ref=lift.at[rows, columns],
            dst_ref=received.at[level - 1, rows, columns],
            send_sem=send_sem.at[level - 1, piece],
            recv_sem=recv_sem.at[level - 1, piece],
            device_id=partner_of(level),
            device_id_type=MESH,
        )

    core = lax.axis_index("dev") % 2
    mine = pl.ds(pl.multiple_of(core * HALF, HALF), HALF)
    sides, outer = slice(RANK, WIDE), slice(HALF, RANK)

    def crowded(level):
        return (level - 5) * (level - 6) == 0

    def roomy(level):
        return (level - 5) * (level - 6) != 0


    def exchange_half(level, columns, slot):
        return pltpu.make_async_remote_copy(
            src_ref=lift.at[mine, columns],
            dst_ref=received.at[level - 1, mine, columns],
            send_sem=send_sem.at[level - 1, slot],
            recv_sem=recv_sem.at[level - 1, slot],
            device_id=partner_of(level),
            device_id_type=MESH,
        )

    def relay_half(level, columns, slot):
        return pltpu.make_async_remote_copy(
            src_ref=received.at[level - 1, mine, columns],
            dst_ref=received.at[level - 1, mine, columns],
            send_sem=send_sem.at[level - 1, slot],
            recv_sem=recv_sem.at[level - 1, slot],
            device_id=partner_of(1),
            device_id_type=MESH,
        )

    loaded[0].wait()
    basis_parts = halves(basis[...])
    for band, copy in zip(bands, loaded[1:]):
        copy.wait()
        leaf_w[band, :] = dot_parts(halves(inverse[band, :]), basis_parts)
    for piece in range(3):
        rows, columns = BLOCKS[piece]
        lift[rows, columns] = dot_tn(basis[:, rows], leaf_w[:, columns])
        if piece == 0:
            pl.semaphore_wait(barrier, LEVELS)
        exchange(1, piece).start()
        if piece == 0:
            exchange(1, 4).start()
    for copy in loaded[4:]:
        copy.wait()
    rows = lax.broadcasted_iota(jnp.int32, (LEAF, LEAF), 0)
    hot[...] = jnp.where(rows == order_ref[...], 1.0, 0.0).astype(BF)
    stacked = jnp.concatenate([p.astype(BF) for p in parts_of(loads[...])], axis=1)
    leaf_y[...] = whole(dot_tn_exact(hot[...], stacked))

    def leaf_loads():
        leaf_y[...] = dot(inverse[...], leaf_y[...])
        lift[:, RANK:] = dot_tn(basis[...], leaf_y[...])
        exchange(1, 3).start()

    def to_initial_order():
        stacked = jnp.concatenate([p.astype(BF) for p in parts_of(leaf_y[...])], axis=1)
        leaf_y[...] = whole(jnp.dot(hot[...], stacked, preferred_element_type=F32))
        stacked = jnp.concatenate([p.astype(BF) for p in parts_of(leaf_w[...])], axis=1)
        leaf_w[...] = whole(jnp.dot(hot[...], stacked, preferred_element_type=F32))

    def node(level, carry):
        slot = level - 1
        base = slot * RANK
        top = pl.ds(pl.multiple_of(base, RANK), HALF)
        bottom = pl.ds(pl.multiple_of(base + HALF, HALF), HALF)

        def joined(rows, columns):
            return lift[rows, columns] + received[slot, rows, columns]

        exchange(level, 0).wait_recv()
        half = HALF // 2
        own = block[top, 0:HALF] + lift[0:HALF, 0:HALF]
        low[0:half, :] = own[:half] + received[slot, 0:half, 0:HALF]
        low[half:HALF, :] = own[half:]

        def lower_rows():
            exchange(level, 4).wait_recv()
            lane = lax.broadcasted_iota(jnp.int32, (half, HALF), 1)
            came = received[slot, half:HALF, 0:HALF]
            low[half:HALF, :] = low[half:HALF, :] + jnp.where(lane >= LATE, came, 0.0)

        sweep(low, lower_rows)

        @pl.when(roomy(level))
        def _():
            exchange(level, 1).wait_recv()
            exchange(level, 2).wait_recv()

        @pl.when(crowded(level))
        def _():
            exchange_half(level, outer, 1).wait_recv()
            relay_half(level, outer, 2).start()
            relay_half(level, outer, 2).wait()

        first = -low[...]
        cross = block[top, HALF:RANK] + joined(*PIECES[1])
        through = dot(first, cross)
        high[...] = block[bottom, HALF:RANK] + joined(*PIECES[2]) - dot_tn(cross, through)
        link_low = link[top, :]
        solved_low = dot(first, link_low)
        rest = link[bottom, :] - dot_tn(cross, solved_low)
        lifted = [
            dot_tn(link_low[:, rows], solved_low[:, columns]) for rows, columns in BLOCKS
        ]
        rest_parts, turned_parts = halves(rest), halves(rest.T)
        sweep(high)
        second = -high[...]
        exchange(level, 0).wait_send()
        exchange(level, 4).wait_send()

        @pl.when(roomy(level))
        def _():
            exchange(level, 1).wait_send()
            exchange(level, 2).wait_send()

        @pl.when(crowded(level))
        def _():
            exchange_half(level, outer, 1).wait_send()
            exchange_half(level, sides, 3).wait_recv()
            relay_half(level, sides, 5).start()

        @pl.when(level < LEVELS)
        def _():
            inverse_parts = halves(second)
            near = dot_parts(inverse_parts, [p[:, :HALF] for p in rest_parts])
            near_parts = halves(near)
            lift[0:HALF, 0:HALF] = lifted[0] + dot_parts([p[:HALF] for p in turned_parts], near_parts)
            exchange(level + 1, 0).start()
            far = dot_parts(inverse_parts, [p[:, HALF:] for p in rest_parts])
            exchange(level + 1, 4).start()
            both = dot_parts(turned_parts, halves(far))
            lift[0:HALF, HALF:RANK] = lifted[1] + both[:HALF]
            lift[HALF:RANK, HALF:RANK] = lifted[2] + both[HALF:]

            @pl.when(roomy(level + 1))
            def _():
                exchange(level + 1, 1).start()
                exchange(level + 1, 2).start()

            @pl.when(crowded(level + 1))
            def _():
                exchange_half(level + 1, outer, 1).start()

            gain[slot, HALF:RANK, 0:HALF] = near
            gain[slot, HALF:RANK, HALF:RANK] = far

        pl.when(level == 1)(leaf_loads)

        pl.when(level == 5)(to_initial_order)

        @pl.when(level < LEVELS)
        def _():
            gain[slot, 0:HALF, :] = solved_low - dot(through, gain[slot, HALF:RANK, :])

        @pl.when(roomy(level))
        def _():
            exchange(level, 3).wait()

        @pl.when(crowded(level))
        def _():
            relay_half(level, sides, 5).wait()
            exchange_half(level, sides, 3).wait_send()

        sign = 2.0 * (level % 2).astype(F32) - 1.0
        target = sign * joined(*PIECES[3])
        part_low = dot(first, target[:HALF])
        part_rest = target[HALF:] - dot_tn(cross, part_low)
        part_high = dot(second, part_rest)

        @pl.when(level < LEVELS)
        def _():
            lift[:, RANK:] = dot_tn(link_low, part_low) + dot_tn(rest, part_high)

            @pl.when(roomy(level + 1))
            def _():
                exchange(level + 1, 3).start()

            @pl.when(crowded(level + 1))
            def _():
                exchange_half(level + 1, sides, 3).start()

        part[slot, 0:HALF, :] = part_low - dot(through, part_high)
        part[slot, HALF:RANK, :] = part_high
        return carry

    lax.fori_loop(1, LEVELS + 1, node, 0)

    value[...] = part[LEVELS - 1]

    def down(step, carry):
        level = LEVELS - 1 - step
        sign = 1.0 - 2.0 * (level % 2).astype(F32)
        value[...] = part[level - 1] - sign * dot(gain[level - 1], value[...])
        return carry

    lax.fori_loop(0, LEVELS - 1, down, 0)
    result[...] = leaf_y[...] - dot(leaf_w[...], value[...])
    done = pltpu.make_async_copy(result, out_hbm, out_sem)
    done.start()
    done.wait()


def shards(leaf_inverse, leaf_basis, node_block, node_link, loads, order):
    hbm = pl.BlockSpec(memory_space=pltpu.HBM)
    return pl.pallas_call(
        kernel,
        out_shape=jax.ShapeDtypeStruct(loads.shape, F32),
        in_specs=[hbm] * 5 + [pl.BlockSpec(memory_space=pltpu.VMEM)],
        out_specs=hbm,
        scratch_shapes=[
            pltpu.VMEM((LEAF, LEAF), F32),
            pltpu.VMEM((LEAF, RANK), F32),
            pltpu.VMEM((LEVELS * RANK, RANK), F32),
            pltpu.VMEM((LEVELS * RANK, RANK), F32),
            pltpu.VMEM((LEAF, NRHS), F32),
            pltpu.VMEM((LEAF, LEAF), BF),
            pltpu.VMEM((LEAF, RANK), F32),
            pltpu.VMEM((LEAF, NRHS), F32),
            pltpu.VMEM((RANK, WIDE), F32),
            pltpu.VMEM((LEVELS, RANK, WIDE), F32),
            pltpu.VMEM((LEVELS, RANK, RANK), F32),
            pltpu.VMEM((LEVELS, RANK, NRHS), F32),
            pltpu.VMEM((RANK, NRHS), F32),
            pltpu.VMEM((HALF, HALF), F32),
            pltpu.VMEM((HALF, HALF), F32),
            pltpu.VMEM((LEAF, NRHS), F32),
            pltpu.SemaphoreType.DMA((7,)),
            pltpu.SemaphoreType.DMA((LEVELS, 6)),
            pltpu.SemaphoreType.DMA((LEVELS, 6)),
            pltpu.SemaphoreType.DMA,
        ],
        compiler_params=pltpu.CompilerParams(
            collective_id=0, has_side_effects=True, vmem_limit_bytes=63 * 1024 * 1024
        ),
        cost_estimate=pl.CostEstimate(flops=4_000_000_000, bytes_accessed=8_000_000, transcendentals=0),
    )(leaf_inverse, leaf_basis, node_block, node_link, loads, order)


def solution(mesh):
    spec = P(("grp", "dev"), None)
    return jax.shard_map(shards, mesh=mesh, in_specs=(spec,) * 6, out_specs=spec, check_vma=False)
```

```python
import functools
import jax
import jax.numpy as jnp
from jax import lax
from jax.experimental import pallas as pl
from jax.experimental.pallas import tpu as pltpu
from jax.sharding import PartitionSpec as P

BF = jnp.bfloat16
F32 = jnp.float32
MESH = pl.DeviceIdType.MESH
HALF = 128
RANK = 256
NRHS = 128
LEAF = 768
LEVELS = 8
AHEAD = 2
LATE = 48
WIDE = RANK + NRHS
TERMS = ((0, 0), (0, 1), (1, 0), (0, 2), (2, 0), (1, 1))


def halves(x):
    high = x.astype(BF)
    return high, (x - high.astype(F32)).astype(BF)


def dot_parts(a, b):
    one = lambda p, q: jnp.dot(p, q, preferred_element_type=F32)
    return one(a[0], b[0]) + (one(a[0], b[1]) + one(a[1], b[0]))


def dot(a, b):
    return dot_parts(halves(a), halves(b))


def dot_tn(a, b):
    ah, al = halves(a)
    bh, bl = halves(b)
    one = lambda p, q: lax.dot_general(p, q, (((0,), (0,)), ((), ())), preferred_element_type=F32)
    return one(ah, bh) + (one(ah, bl) + one(al, bh))


def dot_tn_exact(a, b):
    return lax.dot_general(a, b, (((0,), (0,)), ((), ())), preferred_element_type=F32)


def whole(x):
    size = x.shape[1] // 3
    return (x[:, :size] + x[:, size : 2 * size]) + x[:, 2 * size :]


def parts_of(x):
    high = x.astype(BF).astype(F32)
    rest = x - high
    mid = rest.astype(BF).astype(F32)
    return (high, mid, rest - mid)


def rank_product(rows, solved):
    a, b = parts_of(rows), parts_of(solved)
    left = jnp.concatenate([a[i] for i, _ in TERMS], axis=0).astype(BF)
    right = jnp.concatenate([b[j] for _, j in TERMS], axis=0).astype(BF)
    return lax.dot_general(left, right, (((0,), (0,)), ((), ())), preferred_element_type=F32)


def sweep(a_ref, late=None):
    size = a_ref.shape[0]
    groups = size // 8
    tile = (8, size)
    lane = lax.broadcasted_iota(jnp.int32, tile, 1)
    sub = lax.broadcasted_iota(jnp.int32, tile, 0)

    def spread(v, i):
        return jnp.broadcast_to(v[i : i + 1, :], tile)

    def column(v, j):
        return jnp.take_along_axis(v, jnp.full(tile, j, jnp.int32), axis=1)

    def updated(old, first, row, columns=None):
        columns = columns or [column(old, first + i) for i in range(8)]
        terms = [c * r for c, r in zip(columns, row)]
        while len(terms) > 1:
            terms = [terms[q] + terms[q + 1] for q in range(0, len(terms), 2)]
        here = (lane >= first) & (lane < first + 8)
        return jnp.where(here, 0.0, old) - terms[0]

    near = {g: a_ref[8 * g : 8 * g + 8, :] for g in range(AHEAD + 1)}
    diag = [column(near[0], j) for j in range(8)]
    cross = [column(near[1], j) for j in range(8)]
    lefts, rights, swept = [], [], {}
    for step in range(groups):
        first = 8 * step
        now = near.pop(step)
        here = (lane >= first) & (lane < first + 8)
        more = step + 1 < groups
        entry = {(i, j): spread(diag[j], i) for j in range(8) for i in range(j, 8)}
        row = [
            jnp.where(here, jnp.where(lane == first + i, -1.0, 0.0), spread(now, i))
            for i in range(8)
        ]
        if more:
            diag = [column(near[step + 1], first + 8 + j) for j in range(8)]
            reduced = list(cross)
        lower, pivot = {}, []
        for k in range(8):
            pivot.append(1.0 / entry[k, k])
            for i in range(k + 1, 8):
                lower[i, k] = entry[i, k] * pivot[k]
                for j in range(k + 1, i + 1):
                    entry[i, j] = entry[i, j] - lower[i, k] * entry[j, k]
                if more:
                    reduced[i] = reduced[i] - lower[i, k] * reduced[k]
            for i in range(k + 1, 8):
                row[i] = row[i] - lower[i, k] * row[k]
            if more:
                scaled = reduced[k] * pivot[k]
                diag = [diag[j] - scaled * spread(reduced[k], j) for j in range(8)]
        row = [r * p for r, p in zip(row, pivot)]
        for k in range(7, -1, -1):
            for i in range(k):
                row[i] = row[i] - lower[k, i] * row[k]
        solved = row[7]
        for i in range(7):
            solved = jnp.where(sub == i, row[i], solved)
        reach = step + AHEAD + (1 - step % 2)
        later = {}
        for g in range(step + 1, min(groups, reach + 1)):
            old = near[g] if g in near else a_ref[8 * g : 8 * g + 8, :]
            later[g] = updated(old, first, row, cross if g == step + 1 else None)
        swept = {g: updated(old, first, row) for g, old in swept.items()}
        swept[step] = solved
        lefts.append(now)
        rights = [jnp.where(here, 0.0, r) for r in rights] + [solved]
        if step % 2:
            change = rank_product(jnp.concatenate(lefts, axis=0), jnp.concatenate(rights, axis=0))
            gone = (lane >= first - 8) & (lane < first + 8)
            for g in range(groups):
                rows = slice(8 * g, 8 * g + 8)
                if g in swept:
                    a_ref[rows, :] = swept[g]
                elif g not in later:
                    a_ref[rows, :] = jnp.where(gone, 0.0, a_ref[rows, :]) - change[rows, :]
            lefts, rights, swept = [], [], {}
            if late is not None and first + 8 == LATE:
                late()
        near = later
        if step + 2 < groups:
            cross = [column(near[step + 2], first + 8 + i) for i in range(8)]


PIECES = (
    (slice(0, 64), slice(0, 128)),
    (slice(0, 128), slice(128, 256)),
    (slice(128, 256), slice(128, 256)),
    (slice(0, 256), slice(256, 384)),
    (slice(64, 128), slice(0, 128)),
)
BLOCKS = ((slice(0, 128), slice(0, 128)),) + PIECES[1:3]


def partner_of(level):
    dev, grp = lax.axis_index("dev"), lax.axis_index("grp")
    core, x, z = dev % 2, (dev // 2) % 4, dev // 8
    one = lambda flag, yes, no: jnp.where(flag, yes, no)
    new_core = one(level == 1, 1 - core, core)
    flip_x = x + 1 - 2 * (x % 2)
    new_x = one(level == 2, flip_x, one(level == 3, 3 - x, x))
    flip_z0 = z + 1 - 2 * (z % 2)
    flip_z1 = z + 2 - 4 * ((z // 2) % 2)
    new_z = one(level == 4, flip_z0, one(level == 5, flip_z1, one(level == 6, 7 - z, z)))
    flip_y = grp + 1 - 2 * (grp % 2)
    new_y = one(level == 7, flip_y, one(level == 8, 3 - grp, grp))
    return (new_y, (new_z * 4 + new_x) * 2 + new_core)


def kernel(
    inverse_hbm, basis_hbm, block_hbm, link_hbm, loads_hbm, order_ref, out_hbm,
    inverse, basis, block, link, loads, hot, leaf_w, leaf_y, lift, received, gain, part, value, low, high, result,
    in_sem, send_sem, recv_sem, out_sem,
):
    loaded = []
    bands = [pl.ds(RANK * i, RANK) for i in range(LEAF // RANK)]
    for i, (src, dst) in enumerate(
        [(basis_hbm, basis)]
        + [(inverse_hbm.at[band], inverse.at[band]) for band in bands]
        + [(loads_hbm, loads), (block_hbm, block), (link_hbm, link)]
    ):
        loaded.append(pltpu.make_async_copy(src, dst, in_sem.at[i]))
        loaded[-1].start()
    barrier = pltpu.get_barrier_semaphore()
    for level in range(1, LEVELS + 1):
        pl.semaphore_signal(barrier, inc=1, device_id=partner_of(level), device_id_type=MESH)

    def exchange(level, piece):
        rows, columns = PIECES[piece]
        return pltpu.make_async_remote_copy(
            src_ref=lift.at[rows, columns],
            dst_ref=received.at[level - 1, rows, columns],
            send_sem=send_sem.at[level - 1, piece],
            recv_sem=recv_sem.at[level - 1, piece],
            device_id=partner_of(level),
            device_id_type=MESH,
        )

    core = lax.axis_index("dev") % 2
    mine = pl.ds(pl.multiple_of(core * HALF, HALF), HALF)
    sides, outer = slice(RANK, WIDE), slice(HALF, RANK)

    def crowded(level):
        return (level - 5) * (level - 6) == 0

    def roomy(level):
        return (level - 5) * (level - 6) != 0


    def exchange_half(level, columns, slot):
        return pltpu.make_async_remote_copy(
            src_ref=lift.at[mine, columns],
            dst_ref=received.at[level - 1, mine, columns],
            send_sem=send_sem.at[level - 1, slot],
            recv_sem=recv_sem.at[level - 1, slot],
            device_id=partner_of(level),
            device_id_type=MESH,
        )

    def relay_half(level, columns, slot):
        return pltpu.make_async_remote_copy(
            src_ref=received.at[level - 1, mine, columns],
            dst_ref=received.at[level - 1, mine, columns],
            send_sem=send_sem.at[level - 1, slot],
            recv_sem=recv_sem.at[level - 1, slot],
            device_id=partner_of(1),
            device_id_type=MESH,
        )

    loaded[0].wait()
    basis_parts = halves(basis[...])
    for band, copy in zip(bands, loaded[1:]):
        copy.wait()
        leaf_w[band, :] = dot_parts(halves(inverse[band, :]), basis_parts)
    for piece in range(3):
        rows, columns = BLOCKS[piece]
        lift[rows, columns] = dot_tn(basis[:, rows], leaf_w[:, columns])
        if piece == 0:
            pl.semaphore_wait(barrier, LEVELS)
        exchange(1, piece).start()
        if piece == 0:
            exchange(1, 4).start()
    for copy in loaded[4:]:
        copy.wait()
    rows = lax.broadcasted_iota(jnp.int32, (LEAF, LEAF), 0)
    hot[...] = jnp.where(rows == order_ref[...], 1.0, 0.0).astype(BF)
    stacked = jnp.concatenate([p.astype(BF) for p in parts_of(loads[...])], axis=1)
    leaf_y[...] = whole(dot_tn_exact(hot[...], stacked))

    def leaf_loads():
        leaf_y[...] = dot(inverse[...], leaf_y[...])
        lift[:, RANK:] = dot_tn(basis[...], leaf_y[...])
        exchange(1, 3).start()

    def to_initial_order():
        stacked = jnp.concatenate([p.astype(BF) for p in parts_of(leaf_y[...])], axis=1)
        leaf_y[...] = whole(jnp.dot(hot[...], stacked, preferred_element_type=F32))
        stacked = jnp.concatenate([p.astype(BF) for p in parts_of(leaf_w[...])], axis=1)
        leaf_w[...] = whole(jnp.dot(hot[...], stacked, preferred_element_type=F32))

    def node(level, carry):
        slot = level - 1
        base = slot * RANK
        top = pl.ds(pl.multiple_of(base, RANK), HALF)
        bottom = pl.ds(pl.multiple_of(base + HALF, HALF), HALF)

        def joined(rows, columns):
            return lift[rows, columns] + received[slot, rows, columns]

        exchange(level, 0).wait_recv()
        half = HALF // 2
        own = block[top, 0:HALF] + lift[0:HALF, 0:HALF]
        low[0:half, :] = own[:half] + received[slot, 0:half, 0:HALF]
        low[half:HALF, :] = own[half:]

        def lower_rows():
            exchange(level, 4).wait_recv()
            lane = lax.broadcasted_iota(jnp.int32, (half, HALF), 1)
            came = received[slot, half:HALF, 0:HALF]
            low[half:HALF, :] = low[half:HALF, :] + jnp.where(lane >= LATE, came, 0.0)

        sweep(low, lower_rows)

        @pl.when(roomy(level))
        def _():
            exchange(level, 1).wait_recv()
            exchange(level, 2).wait_recv()

        @pl.when(crowded(level))
        def _():
            exchange_half(level, outer, 1).wait_recv()
            relay_half(level, outer, 2).start()
            relay_half(level, outer, 2).wait_recv()

        first = -low[...]
        cross = block[top, HALF:RANK] + joined(*PIECES[1])
        through = dot(first, cross)
        high[...] = block[bottom, HALF:RANK] + joined(*PIECES[2]) - dot_tn(cross, through)
        link_low = link[top, :]
        solved_low = dot(first, link_low)
        rest = link[bottom, :] - dot_tn(cross, solved_low)
        lifted = [
            dot_tn(link_low[:, rows], solved_low[:, columns]) for rows, columns in BLOCKS
        ]
        rest_parts, turned_parts = halves(rest), halves(rest.T)
        sweep(high)
        second = -high[...]
        exchange(level, 0).wait_send()
        exchange(level, 4).wait_send()

        @pl.when(roomy(level))
        def _():
            exchange(level, 1).wait_send()
            exchange(level, 2).wait_send()

        @pl.when(crowded(level))
        def _():
            relay_half(level, outer, 2).wait_send()
            exchange_half(level, outer, 1).wait_send()
            exchange_half(level, sides, 3).wait_recv()
            relay_half(level, sides, 5).start()

        @pl.when(level < LEVELS)
        def _():
            inverse_parts = halves(second)
            near = dot_parts(inverse_parts, [p[:, :HALF] for p in rest_parts])
            near_parts = halves(near)
            lift[0:HALF, 0:HALF] = lifted[0] + dot_parts([p[:HALF] for p in turned_parts], near_parts)
            exchange(level + 1, 0).start()
            far = dot_parts(inverse_parts, [p[:, HALF:] for p in rest_parts])
            exchange(level + 1, 4).start()
            both = dot_parts(turned_parts, halves(far))
            lift[0:HALF, HALF:RANK] = lifted[1] + both[:HALF]
            lift[HALF:RANK, HALF:RANK] = lifted[2] + both[HALF:]

            @pl.when(roomy(level + 1))
            def _():
                exchange(level + 1, 1).start()
                exchange(level + 1, 2).start()

            @pl.when(crowded(level + 1))
            def _():
                exchange_half(level + 1, outer, 1).start()

            gain[slot, HALF:RANK, 0:HALF] = near
            gain[slot, HALF:RANK, HALF:RANK] = far

        pl.when(level == 1)(leaf_loads)

        pl.when(level == 5)(to_initial_order)

        @pl.when(level < LEVELS)
        def _():
            gain[slot, 0:HALF, :] = solved_low - dot(through, gain[slot, HALF:RANK, :])

        @pl.when(roomy(level))
        def _():
            exchange(level, 3).wait_recv()

        @pl.when(crowded(level))
        def _():
            relay_half(level, sides, 5).wait_recv()

        sign = 2.0 * (level % 2).astype(F32) - 1.0
        target = sign * joined(*PIECES[3])
        part_low = dot(first, target[:HALF])
        part_rest = target[HALF:] - dot_tn(cross, part_low)
        part_high = dot(second, part_rest)

        @pl.when(roomy(level))
        def _():
            exchange(level, 3).wait_send()

        @pl.when(crowded(level))
        def _():
            relay_half(level, sides, 5).wait_send()
            exchange_half(level, sides, 3).wait_send()

        @pl.when(level < LEVELS)
        def _():
            lift[:, RANK:] = dot_tn(link_low, part_low) + dot_tn(rest, part_high)

            @pl.when(roomy(level + 1))
            def _():
                exchange(level + 1, 3).start()

            @pl.when(crowded(level + 1))
            def _():
                exchange_half(level + 1, sides, 3).start()

        part[slot, 0:HALF, :] = part_low - dot(through, part_high)
        part[slot, HALF:RANK, :] = part_high
        return carry

    lax.fori_loop(1, LEVELS + 1, node, 0)

    value[...] = part[LEVELS - 1]

    def down(step, carry):
        level = LEVELS - 1 - step
        sign = 1.0 - 2.0 * (level % 2).astype(F32)
        value[...] = part[level - 1] - sign * dot(gain[level - 1], value[...])
        return carry

    lax.fori_loop(0, LEVELS - 1, down, 0)
    result[...] = leaf_y[...] - dot(leaf_w[...], value[...])
    done = pltpu.make_async_copy(result, out_hbm, out_sem)
    done.start()
    done.wait()


def shards(leaf_inverse, leaf_basis, node_block, node_link, loads, order):
    hbm = pl.BlockSpec(memory_space=pltpu.HBM)
    return pl.pallas_call(
        kernel,
        out_shape=jax.ShapeDtypeStruct(loads.shape, F32),
        in_specs=[hbm] * 5 + [pl.BlockSpec(memory_space=pltpu.VMEM)],
        out_specs=hbm,
        scratch_shapes=[
            pltpu.VMEM((LEAF, LEAF), F32),
            pltpu.VMEM((LEAF, RANK), F32),
            pltpu.VMEM((LEVELS * RANK, RANK), F32),
            pltpu.VMEM((LEVELS * RANK, RANK), F32),
            pltpu.VMEM((LEAF, NRHS), F32),
            pltpu.VMEM((LEAF, LEAF), BF),
            pltpu.VMEM((LEAF, RANK), F32),
            pltpu.VMEM((LEAF, NRHS), F32),
            pltpu.VMEM((RANK, WIDE), F32),
            pltpu.VMEM((LEVELS, RANK, WIDE), F32),
            pltpu.VMEM((LEVELS, RANK, RANK), F32),
            pltpu.VMEM((LEVELS, RANK, NRHS), F32),
            pltpu.VMEM((RANK, NRHS), F32),
            pltpu.VMEM((HALF, HALF), F32),
            pltpu.VMEM((HALF, HALF), F32),
            pltpu.VMEM((LEAF, NRHS), F32),
            pltpu.SemaphoreType.DMA((7,)),
            pltpu.SemaphoreType.DMA((LEVELS, 6)),
            pltpu.SemaphoreType.DMA((LEVELS, 6)),
            pltpu.SemaphoreType.DMA,
        ],
        compiler_params=pltpu.CompilerParams(
            collective_id=0, has_side_effects=True, vmem_limit_bytes=63 * 1024 * 1024
        ),
        cost_estimate=pl.CostEstimate(flops=4_000_000_000, bytes_accessed=8_000_000, transcendentals=0),
    )(leaf_inverse, leaf_basis, node_block, node_link, loads, order)


def solution(mesh):
    spec = P(("grp", "dev"), None)
    return jax.shard_map(shards, mesh=mesh, in_specs=(spec,) * 6, out_specs=spec, check_vma=False)
```

```python
import functools
import jax
import jax.numpy as jnp
from jax import lax
from jax.experimental import pallas as pl
from jax.experimental.pallas import tpu as pltpu
from jax.sharding import PartitionSpec as P

BF = jnp.bfloat16
F32 = jnp.float32
MESH = pl.DeviceIdType.MESH
HALF = 128
RANK = 256
NRHS = 128
LEAF = 768
LEVELS = 8
AHEAD = 2
LATE = 48
WIDE = RANK + NRHS
TERMS = ((0, 0), (0, 1), (1, 0), (0, 2), (2, 0), (1, 1))


def halves(x):
    high = x.astype(BF)
    return high, (x - high.astype(F32)).astype(BF)


def dot_parts(a, b):
    one = lambda p, q: jnp.dot(p, q, preferred_element_type=F32)
    return one(a[0], b[0]) + (one(a[0], b[1]) + one(a[1], b[0]))


def dot(a, b):
    return dot_parts(halves(a), halves(b))


def dot_tn(a, b):
    ah, al = halves(a)
    bh, bl = halves(b)
    one = lambda p, q: lax.dot_general(p, q, (((0,), (0,)), ((), ())), preferred_element_type=F32)
    return one(ah, bh) + (one(ah, bl) + one(al, bh))


def dot_tn_exact(a, b):
    return lax.dot_general(a, b, (((0,), (0,)), ((), ())), preferred_element_type=F32)


def whole(x):
    size = x.shape[1] // 3
    return (x[:, :size] + x[:, size : 2 * size]) + x[:, 2 * size :]


def parts_of(x):
    high = x.astype(BF).astype(F32)
    rest = x - high
    mid = rest.astype(BF).astype(F32)
    return (high, mid, rest - mid)


def rank_product(rows, solved):
    a, b = parts_of(rows), parts_of(solved)
    left = jnp.concatenate([a[i] for i, _ in TERMS], axis=0).astype(BF)
    right = jnp.concatenate([b[j] for _, j in TERMS], axis=0).astype(BF)
    return lax.dot_general(left, right, (((0,), (0,)), ((), ())), preferred_element_type=F32)


def sweep(a_ref, late=None):
    size = a_ref.shape[0]
    groups = size // 8
    tile = (8, size)
    lane = lax.broadcasted_iota(jnp.int32, tile, 1)
    sub = lax.broadcasted_iota(jnp.int32, tile, 0)

    def spread(v, i):
        return jnp.broadcast_to(v[i : i + 1, :], tile)

    def column(v, j):
        return jnp.take_along_axis(v, jnp.full(tile, j, jnp.int32), axis=1)

    def updated(old, first, row, columns=None):
        columns = columns or [column(old, first + i) for i in range(8)]
        terms = [c * r for c, r in zip(columns, row)]
        while len(terms) > 1:
            terms = [terms[q] + terms[q + 1] for q in range(0, len(terms), 2)]
        here = (lane >= first) & (lane < first + 8)
        return jnp.where(here, 0.0, old) - terms[0]

    near = {g: a_ref[8 * g : 8 * g + 8, :] for g in range(AHEAD + 1)}
    diag = [column(near[0], j) for j in range(8)]
    cross = [column(near[1], j) for j in range(8)]
    lefts, rights, swept = [], [], {}
    for step in range(groups):
        first = 8 * step
        now = near.pop(step)
        here = (lane >= first) & (lane < first + 8)
        more = step + 1 < groups
        entry = {(i, j): spread(diag[j], i) for j in range(8) for i in range(j, 8)}
        row = [
            jnp.where(here, jnp.where(lane == first + i, -1.0, 0.0), spread(now, i))
            for i in range(8)
        ]
        if more:
            diag = [column(near[step + 1], first + 8 + j) for j in range(8)]
            reduced = list(cross)
        lower, pivot = {}, []
        for k in range(8):
            pivot.append(1.0 / entry[k, k])
            for i in range(k + 1, 8):
                lower[i, k] = entry[i, k] * pivot[k]
                for j in range(k + 1, i + 1):
                    entry[i, j] = entry[i, j] - lower[i, k] * entry[j, k]
                if more:
                    reduced[i] = reduced[i] - lower[i, k] * reduced[k]
            for i in range(k + 1, 8):
                row[i] = row[i] - lower[i, k] * row[k]
            if more:
                scaled = reduced[k] * pivot[k]
                diag = [diag[j] - scaled * spread(reduced[k], j) for j in range(8)]
        row = [r * p for r, p in zip(row, pivot)]
        for k in range(7, -1, -1):
            for i in range(k):
                row[i] = row[i] - lower[k, i] * row[k]
        solved = row[7]
        for i in range(7):
            solved = jnp.where(sub == i, row[i], solved)
        reach = step + AHEAD + (1 - step % 2)
        later = {}
        for g in range(step + 1, min(groups, reach + 1)):
            old = near[g] if g in near else a_ref[8 * g : 8 * g + 8, :]
            later[g] = updated(old, first, row, cross if g == step + 1 else None)
        swept = {g: updated(old, first, row) for g, old in swept.items()}
        swept[step] = solved
        lefts.append(now)
        rights = [jnp.where(here, 0.0, r) for r in rights] + [solved]
        if step % 2:
            change = rank_product(jnp.concatenate(lefts, axis=0), jnp.concatenate(rights, axis=0))
            gone = (lane >= first - 8) & (lane < first + 8)
            for g in range(groups):
                rows = slice(8 * g, 8 * g + 8)
                if g in swept:
                    a_ref[rows, :] = swept[g]
                elif g not in later:
                    a_ref[rows, :] = jnp.where(gone, 0.0, a_ref[rows, :]) - change[rows, :]
            lefts, rights, swept = [], [], {}
            if late is not None and first + 8 == LATE:
                late()
        near = later
        if step + 2 < groups:
            cross = [column(near[step + 2], first + 8 + i) for i in range(8)]


PIECES = (
    (slice(0, 64), slice(0, 128)),
    (slice(0, 128), slice(128, 256)),
    (slice(128, 256), slice(128, 256)),
    (slice(0, 256), slice(256, 384)),
    (slice(64, 128), slice(0, 128)),
)
BLOCKS = ((slice(0, 128), slice(0, 128)),) + PIECES[1:3]


def partner_of(level):
    dev, grp = lax.axis_index("dev"), lax.axis_index("grp")
    core, x, z = dev % 2, (dev // 2) % 4, dev // 8
    one = lambda flag, yes, no: jnp.where(flag, yes, no)
    new_core = one(level == 1, 1 - core, core)
    flip_x = x + 1 - 2 * (x % 2)
    new_x = one(level == 2, flip_x, one(level == 3, 3 - x, x))
    flip_z0 = z + 1 - 2 * (z % 2)
    flip_z1 = z + 2 - 4 * ((z // 2) % 2)
    new_z = one(level == 4, flip_z0, one(level == 5, flip_z1, one(level == 6, 7 - z, z)))
    flip_y = grp + 1 - 2 * (grp % 2)
    new_y = one(level == 7, flip_y, one(level == 8, 3 - grp, grp))
    return (new_y, (new_z * 4 + new_x) * 2 + new_core)


def kernel(
    inverse_hbm, basis_hbm, block_hbm, link_hbm, loads_hbm, order_ref, out_hbm,
    inverse, basis, block, link, loads, hot, leaf_w, leaf_y, lift, received, gain, part, value, low, high, result,
    in_sem, send_sem, recv_sem, out_sem,
):
    loaded = []
    bands = [pl.ds(RANK * i, RANK) for i in range(LEAF // RANK)]
    for i, (src, dst) in enumerate(
        [(basis_hbm, basis)]
        + [(inverse_hbm.at[band], inverse.at[band]) for band in bands]
        + [(loads_hbm, loads), (block_hbm, block), (link_hbm, link)]
    ):
        loaded.append(pltpu.make_async_copy(src, dst, in_sem.at[i]))
        loaded[-1].start()
    barrier = pltpu.get_barrier_semaphore()
    for level in range(1, LEVELS + 1):
        pl.semaphore_signal(barrier, inc=1, device_id=partner_of(level), device_id_type=MESH)

    def exchange(level, piece):
        rows, columns = PIECES[piece]
        return pltpu.make_async_remote_copy(
            src_ref=lift.at[rows, columns],
            dst_ref=received.at[level - 1, rows, columns],
            send_sem=send_sem.at[level - 1, piece],
            recv_sem=recv_sem.at[level - 1, piece],
            device_id=partner_of(level),
            device_id_type=MESH,
        )

    core = lax.axis_index("dev") % 2
    mine = pl.ds(pl.multiple_of(core * HALF, HALF), HALF)
    sides, outer = slice(RANK, WIDE), slice(HALF, RANK)

    def crowded(level):
        return (level - 5) * (level - 6) == 0

    def roomy(level):
        return (level - 5) * (level - 6) != 0


    def exchange_half(level, columns, slot):
        return pltpu.make_async_remote_copy(
            src_ref=lift.at[mine, columns],
            dst_ref=received.at[level - 1, mine, columns],
            send_sem=send_sem.at[level - 1, slot],
            recv_sem=recv_sem.at[level - 1, slot],
            device_id=partner_of(level),
            device_id_type=MESH,
        )

    def relay_half(level, columns, slot):
        return pltpu.make_async_remote_copy(
            src_ref=received.at[level - 1, mine, columns],
            dst_ref=received.at[level - 1, mine, columns],
            send_sem=send_sem.at[level - 1, slot],
            recv_sem=recv_sem.at[level - 1, slot],
            device_id=partner_of(1),
            device_id_type=MESH,
        )

    loaded[0].wait()
    basis_parts = halves(basis[...])
    for band, copy in zip(bands, loaded[1:]):
        copy.wait()
        leaf_w[band, :] = dot_parts(halves(inverse[band, :]), basis_parts)
    for piece in range(3):
        rows, columns = BLOCKS[piece]
        lift[rows, columns] = dot_tn(basis[:, rows], leaf_w[:, columns])
        if piece == 0:
            pl.semaphore_wait(barrier, LEVELS)
        exchange(1, piece).start()
        if piece == 0:
            exchange(1, 4).start()
    for copy in loaded[4:]:
        copy.wait()
    rows = lax.broadcasted_iota(jnp.int32, (LEAF, LEAF), 0)
    hot[...] = jnp.where(rows == order_ref[...], 1.0, 0.0).astype(BF)
    stacked = jnp.concatenate([p.astype(BF) for p in parts_of(loads[...])], axis=1)
    leaf_y[...] = whole(dot_tn_exact(hot[...], stacked))

    def leaf_loads():
        leaf_y[...] = dot(inverse[...], leaf_y[...])
        lift[:, RANK:] = dot_tn(basis[...], leaf_y[...])
        exchange(1, 3).start()

    def to_initial_order():
        stacked = jnp.concatenate([p.astype(BF) for p in parts_of(leaf_y[...])], axis=1)
        leaf_y[...] = whole(jnp.dot(hot[...], stacked, preferred_element_type=F32))
        stacked = jnp.concatenate([p.astype(BF) for p in parts_of(leaf_w[...])], axis=1)
        leaf_w[...] = whole(jnp.dot(hot[...], stacked, preferred_element_type=F32))

    def node(level, carry):
        slot = level - 1
        base = slot * RANK
        top = pl.ds(pl.multiple_of(base, RANK), HALF)
        bottom = pl.ds(pl.multiple_of(base + HALF, HALF), HALF)

        def joined(rows, columns):
            return lift[rows, columns] + received[slot, rows, columns]

        exchange(level, 0).wait_recv()
        half = HALF // 2
        own = block[top, 0:HALF] + lift[0:HALF, 0:HALF]
        low[0:half, :] = own[:half] + received[slot, 0:half, 0:HALF]
        low[half:HALF, :] = own[half:]

        def lower_rows():
            exchange(level, 4).wait_recv()
            lane = lax.broadcasted_iota(jnp.int32, (half, HALF), 1)
            came = received[slot, half:HALF, 0:HALF]
            low[half:HALF, :] = low[half:HALF, :] + jnp.where(lane >= LATE, came, 0.0)

        sweep(low, lower_rows)

        @pl.when(roomy(level))
        def _():
            exchange(level, 1).wait_recv()

        @pl.when(crowded(level))
        def _():
            exchange_half(level, outer, 1).wait_recv()
            relay_half(level, outer, 2).start()
            relay_half(level, outer, 2).wait_recv()

        first = -low[...]
        cross = block[top, HALF:RANK] + joined(*PIECES[1])
        through = dot(first, cross)

        @pl.when(roomy(level))
        def _():
            exchange(level, 2).wait_recv()

        high[...] = block[bottom, HALF:RANK] + joined(*PIECES[2]) - dot_tn(cross, through)
        link_low = link[top, :]
        solved_low = dot(first, link_low)
        rest = link[bottom, :] - dot_tn(cross, solved_low)
        lifted = [
            dot_tn(link_low[:, rows], solved_low[:, columns]) for rows, columns in BLOCKS
        ]
        rest_parts, turned_parts = halves(rest), halves(rest.T)
        sweep(high)
        second = -high[...]
        exchange(level, 0).wait_send()
        exchange(level, 4).wait_send()

        @pl.when(roomy(level))
        def _():
            exchange(level, 1).wait_send()
            exchange(level, 2).wait_send()

        @pl.when(crowded(level))
        def _():
            relay_half(level, outer, 2).wait_send()
            exchange_half(level, outer, 1).wait_send()
            exchange_half(level, sides, 3).wait_recv()
            relay_half(level, sides, 5).start()

        @pl.when(level < LEVELS)
        def _():
            inverse_parts = halves(second)
            near = dot_parts(inverse_parts, [p[:, :HALF] for p in rest_parts])
            near_parts = halves(near)
            lift[0:HALF, 0:HALF] = lifted[0] + dot_parts([p[:HALF] for p in turned_parts], near_parts)
            exchange(level + 1, 0).start()
            far = dot_parts(inverse_parts, [p[:, HALF:] for p in rest_parts])
            exchange(level + 1, 4).start()
            both = dot_parts(turned_parts, halves(far))
            lift[0:HALF, HALF:RANK] = lifted[1] + both[:HALF]
            lift[HALF:RANK, HALF:RANK] = lifted[2] + both[HALF:]

            @pl.when(roomy(level + 1))
            def _():
                exchange(level + 1, 1).start()
                exchange(level + 1, 2).start()

            @pl.when(crowded(level + 1))
            def _():
                exchange_half(level + 1, outer, 1).start()

            gain[slot, HALF:RANK, 0:HALF] = near
            gain[slot, HALF:RANK, HALF:RANK] = far

        pl.when(level == 1)(leaf_loads)

        pl.when(level == 5)(to_initial_order)

        @pl.when(level < LEVELS)
        def _():
            gain[slot, 0:HALF, :] = solved_low - dot(through, gain[slot, HALF:RANK, :])

        @pl.when(roomy(level))
        def _():
            exchange(level, 3).wait_recv()

        @pl.when(crowded(level))
        def _():
            relay_half(level, sides, 5).wait_recv()

        sign = 2.0 * (level % 2).astype(F32) - 1.0
        target = sign * joined(*PIECES[3])
        part_low = dot(first, target[:HALF])
        part_rest = target[HALF:] - dot_tn(cross, part_low)
        part_high = dot(second, part_rest)

        @pl.when(roomy(level))
        def _():
            exchange(level, 3).wait_send()

        @pl.when(crowded(level))
        def _():
            relay_half(level, sides, 5).wait_send()
            exchange_half(level, sides, 3).wait_send()

        @pl.when(level < LEVELS)
        def _():
            lift[:, RANK:] = dot_tn(link_low, part_low) + dot_tn(rest, part_high)

            @pl.when(roomy(level + 1))
            def _():
                exchange(level + 1, 3).start()

            @pl.when(crowded(level + 1))
            def _():
                exchange_half(level + 1, sides, 3).start()

        part[slot, 0:HALF, :] = part_low - dot(through, part_high)
        part[slot, HALF:RANK, :] = part_high
        return carry

    lax.fori_loop(1, LEVELS + 1, node, 0)

    value[...] = part[LEVELS - 1]

    def down(step, carry):
        level = LEVELS - 1 - step
        sign = 1.0 - 2.0 * (level % 2).astype(F32)
        value[...] = part[level - 1] - sign * dot(gain[level - 1], value[...])
        return carry

    lax.fori_loop(0, LEVELS - 1, down, 0)
    result[...] = leaf_y[...] - dot(leaf_w[...], value[...])
    done = pltpu.make_async_copy(result, out_hbm, out_sem)
    done.start()
    done.wait()


def shards(leaf_inverse, leaf_basis, node_block, node_link, loads, order):
    hbm = pl.BlockSpec(memory_space=pltpu.HBM)
    return pl.pallas_call(
        kernel,
        out_shape=jax.ShapeDtypeStruct(loads.shape, F32),
        in_specs=[hbm] * 5 + [pl.BlockSpec(memory_space=pltpu.VMEM)],
        out_specs=hbm,
        scratch_shapes=[
            pltpu.VMEM((LEAF, LEAF), F32),
            pltpu.VMEM((LEAF, RANK), F32),
            pltpu.VMEM((LEVELS * RANK, RANK), F32),
            pltpu.VMEM((LEVELS * RANK, RANK), F32),
            pltpu.VMEM((LEAF, NRHS), F32),
            pltpu.VMEM((LEAF, LEAF), BF),
            pltpu.VMEM((LEAF, RANK), F32),
            pltpu.VMEM((LEAF, NRHS), F32),
            pltpu.VMEM((RANK, WIDE), F32),
            pltpu.VMEM((LEVELS, RANK, WIDE), F32),
            pltpu.VMEM((LEVELS, RANK, RANK), F32),
            pltpu.VMEM((LEVELS, RANK, NRHS), F32),
            pltpu.VMEM((RANK, NRHS), F32),
            pltpu.VMEM((HALF, HALF), F32),
            pltpu.VMEM((HALF, HALF), F32),
            pltpu.VMEM((LEAF, NRHS), F32),
            pltpu.SemaphoreType.DMA((7,)),
            pltpu.SemaphoreType.DMA((LEVELS, 6)),
            pltpu.SemaphoreType.DMA((LEVELS, 6)),
            pltpu.SemaphoreType.DMA,
        ],
        compiler_params=pltpu.CompilerParams(
            collective_id=0, has_side_effects=True, vmem_limit_bytes=63 * 1024 * 1024
        ),
        cost_estimate=pl.CostEstimate(flops=4_000_000_000, bytes_accessed=8_000_000, transcendentals=0),
    )(leaf_inverse, leaf_basis, node_block, node_link, loads, order)


def solution(mesh):
    spec = P(("grp", "dev"), None)
    return jax.shard_map(shards, mesh=mesh, in_specs=(spec,) * 6, out_specs=spec, check_vma=False)
```
